512 devices in a mesh: ctx: 64 (over y, z_hi, x, core), head: 8 (over z_lo).
Axes of the slice: x: 4, y: 4, z: 16 (z_hi: 2, z_lo: 8; z = z_hi * 8 + z_lo), core: 2. Of those that a mesh axis runs over, the one named last changes fastest.
Arguments:
- query_raw: bfloat16 [16384, 5120], P('ctx', 'head'), may hold values from -9 to 9
- key_raw: bfloat16 [16384, 5120], P('ctx', 'head'), may hold values from -9 to 9
- values: bfloat16 [16384, 5120], P('ctx', 'head'), may hold values from -6 to 6
- out_grad: bfloat16 [16384, 5120], P('ctx', 'head'), may hold values from -128 to 128
- query_gain: float32 [5120], P('head'), may hold values from 0.25 to 1.75
- key_gain: float32 [5120], P('head'), may hold values from 0.25 to 1.75
- key_tiles: int32 [128, 4], P('ctx'), may hold values from 0 to 127, as said below
- global_ids: int32 [128], P('ctx'), may hold values from 0 to 16383, as said below
- readers: int32 [64, 64], P('ctx'), may hold values from 0 to 1, as said below
Outputs:
- query_grad: bfloat16 [16384, 5120], P('ctx', 'head')
- key_grad: bfloat16 [16384, 5120], P('ctx', 'head')
- value_grad: bfloat16 [16384, 5120], P('ctx', 'head')
The draws below stay inside these ranges and needn't reach their ends.
Inputs may be any that keep to these rules, and one draw needn't show every extreme that they name: `key_tiles`: row t lists, ascending, the 4 tiles of 4 consecutive tile-frames of 1 tiles; every listed tile lies on an index of ctx at most 1 away from tile t's, and in every draw some tile reads a tile exactly 1 below and some tile one exactly 1 above. `global_ids`: entries c * 2 to (c + 1) * 2 - 1 are distinct ascending tokens of index c of ctx. `readers`: each row has either one 1 or all 64 entries 1; at least one row has all.
All inputs are finite; a program needn't handle non-finite values.
Results may differ from the reference program's by a relative error of at most 0.02.
Values may be sent and summed in bfloat16 or wider, within the bound.
A program may use at most 64 MiB of HBM per device.

```python
import jax
import jax.numpy as jnp
from jax import lax

HEADS = 40
HEAD_DIM = 128
D = 5120
TILE = 128
FRAME_TILES = 1
WIN_FRAMES = 4
REACH = 1
KEYS = 4
TILES_DEV = 2
TOK_DEV = 256
TOKENS = 16384
NT = 128
G_DEV = 2
GLOBAL = 128


def draw_query_raw(key, part):
    position = jnp.arange(D, dtype=jnp.float32)[None, :] / D
    noise = jnp.clip(jax.random.normal(jax.random.fold_in(key, 13), (TOKENS, D)), -5.0, 5.0)
    return (noise * (0.6 + 1.2 * position)).astype(jnp.bfloat16)


def draw_key_raw(key, part):
    position = jnp.arange(D, dtype=jnp.float32)[None, :] / D
    noise = jnp.clip(jax.random.normal(jax.random.fold_in(key, 23), (TOKENS, D)), -5.0, 5.0)
    return (noise * (0.6 + 1.2 * position)).astype(jnp.bfloat16)


def draw_key_tiles(key, part):
    frames_here = TILES_DEV // FRAME_TILES
    frames_all = NT // FRAME_TILES
    devices_count = NT // TILES_DEV
    tile_ids = jnp.arange(NT, dtype=jnp.int32)
    frame_number = tile_ids // FRAME_TILES
    lowest = frame_number - REACH * frames_here
    start_count = 2 * REACH * frames_here - WIN_FRAMES + 2
    start = lowest + jax.random.randint(jax.random.fold_in(key, 31), (NT,), 0, start_count)
    low_device = jax.random.randint(jax.random.fold_in(key, 32), (), REACH, devices_count // 2)
    high_device = jax.random.randint(jax.random.fold_in(key, 33), (), devices_count // 2, devices_count - REACH)
    far_low = low_device * TILES_DEV
    far_high = high_device * TILES_DEV + TILES_DEV - 1
    start = jnp.where(tile_ids == far_low, lowest, start)
    start = jnp.where(tile_ids == far_high, lowest + start_count - 1, start)
    start = jnp.clip(start, 0, frames_all - WIN_FRAMES)
    return (start[:, None] * FRAME_TILES + jnp.arange(KEYS, dtype=jnp.int32)[None, :]).astype(jnp.int32)


def pick_rows(device_key, device_number):
    chosen_rows = jax.random.permutation(device_key, TOK_DEV)[:G_DEV]
    return jnp.sort(chosen_rows).astype(jnp.int32) + device_number * TOK_DEV


def draw_global_ids(key, part):
    devices_count = GLOBAL // G_DEV
    device_keys = jax.random.split(jax.random.fold_in(key, 41), devices_count)
    numbers = jnp.arange(devices_count, dtype=jnp.int32)
    return jax.vmap(pick_rows)(device_keys, numbers).reshape(-1).astype(jnp.int32)


def rank_tiles(device_key):
    return jax.random.permutation(device_key, GLOBAL // G_DEV).astype(jnp.int32)


def draw_readers(key, part):
    devices_count = GLOBAL // G_DEV
    tiles_count = GLOBAL // G_DEV
    ranks = jax.vmap(rank_tiles)(jax.random.split(jax.random.fold_in(key, 51), devices_count))
    heavy = jax.random.randint(jax.random.fold_in(key, 52), (devices_count,), 0, 4) == 0
    busiest = jax.random.randint(jax.random.fold_in(key, 53), (), 0, devices_count)
    heavy = heavy | (jnp.arange(devices_count, dtype=jnp.int32) == busiest)
    counts = jnp.where(heavy, tiles_count, 1)
    return (ranks < counts[:, None]).astype(jnp.int32)


def block_scale(stream_key, shape, cuts, least, high):
    factor_of = 1.0
    for dim, shards_of in cuts:
        draws = jax.random.uniform(jax.random.fold_in(jax.random.fold_in(stream_key, 6), dim), (shards_of,), jnp.float32, least / len(cuts), high / len(cuts))
        factor_of = factor_of * jnp.repeat(jnp.exp(draws), shape[dim] // shards_of).reshape((-1,) + (1,) * (len(shape) - 1 - dim))
    return factor_of


def normal_values(stream_key, dims, deviation, limit, cuts=(), kind=jnp.bfloat16):
    values = deviation * jax.random.normal(stream_key, dims, jnp.float32)
    if cuts:
        values = values * block_scale(stream_key, dims, cuts, -0.22, 0.18)
    return jnp.clip(values, -limit, limit).astype(kind)


def setup_inputs(seed: int = 0) -> dict:
    arg_keys = jax.random.split(jax.random.key(seed), 10)
    query_raw = draw_query_raw(jax.random.fold_in(arg_keys[9], 71), 0)
    key_raw = draw_key_raw(jax.random.fold_in(arg_keys[9], 71), 0)
    values = normal_values(arg_keys[2], (TOKENS, D), 1.0, 6.0, ((0, 64), (1, 8)))
    out_grad = normal_values(arg_keys[3], (TOKENS, D), 24.0, 128.0, ((0, 64), (1, 8)))
    query_gain = jnp.clip(1.0 + 0.15 * jax.random.normal(arg_keys[4], (D,), jnp.float32), 0.25, 1.75)
    key_gain = jnp.clip(1.0 + 0.15 * jax.random.normal(arg_keys[5], (D,), jnp.float32), 0.25, 1.75)
    key_tiles = draw_key_tiles(jax.random.fold_in(arg_keys[9], 71), 0)
    global_ids = draw_global_ids(jax.random.fold_in(arg_keys[9], 71), 0)
    readers = draw_readers(jax.random.fold_in(arg_keys[9], 71), 0)
    return dict(query_raw=query_raw, key_raw=key_raw, values=values, out_grad=out_grad, query_gain=query_gain, key_gain=key_gain, key_tiles=key_tiles, global_ids=global_ids, readers=readers)


EPSILON = 1e-06

def normalize(raw_rows, gain):
    as_float = raw_rows.astype(jnp.float32)
    inverse = lax.rsqrt(lax.optimization_barrier(jnp.mean(as_float * as_float, axis=1, keepdims=True)) + EPSILON)
    normed = lax.optimization_barrier((as_float * inverse * gain).astype(jnp.bfloat16))
    return (as_float, inverse, normed)

def norm_grad(as_float, inverse, scaled):
    coeffs = lax.optimization_barrier(jnp.mean(scaled * as_float, axis=1, keepdims=True))
    return (inverse * scaled - as_float * inverse ** 3 * coeffs).astype(jnp.bfloat16)

def reference(query_raw, key_raw, values, out_grad, query_gain, key_gain, key_tiles, global_ids, readers):
    query_float, query_inv, query_norm = normalize(query_raw, query_gain)
    key_float, key_inv, key_norm = normalize(key_raw, key_gain)
    factor = HEAD_DIM ** (-0.5)
    global_keys = key_norm[global_ids].astype(jnp.float32).reshape(GLOBAL, HEADS, HEAD_DIM)
    global_vals = values[global_ids].astype(jnp.float32).reshape(GLOBAL, HEADS, HEAD_DIM)
    offsets = jnp.arange(TILE, dtype=jnp.int32)

    def one_tile(carry, tile_index):
        key_acc, value_acc = carry
        start = tile_index * TILE
        query_block = lax.dynamic_slice_in_dim(query_norm, start, TILE, 0).astype(jnp.float32).reshape(TILE, HEADS, HEAD_DIM)
        grad_block = lax.dynamic_slice_in_dim(out_grad, start, TILE, 0).astype(jnp.float32).reshape(TILE, HEADS, HEAD_DIM)
        window_rows = (key_tiles[tile_index][:, None] * TILE + offsets[None, :]).reshape(-1).astype(jnp.int32)
        keys_all = jnp.concatenate([key_norm[window_rows].astype(jnp.float32).reshape(-1, HEADS, HEAD_DIM), global_keys], axis=0)
        vals_all = jnp.concatenate([values[window_rows].astype(jnp.float32).reshape(-1, HEADS, HEAD_DIM), global_vals], axis=0)
        live_mask = jnp.concatenate([jnp.ones((KEYS * TILE,), dtype=bool), jnp.repeat(readers[tile_index // TILES_DEV] > 0, G_DEV)])
        scores = jnp.einsum('qhd,khd->hqk', query_block, keys_all) * factor
        scores = jnp.where(live_mask[None, None, :], scores, -jnp.inf)
        largest = lax.optimization_barrier(jnp.max(scores, axis=2, keepdims=True))
        log_total = largest + jnp.log(lax.optimization_barrier(jnp.sum(jnp.exp(scores - largest), axis=2, keepdims=True)))
        probs = jnp.exp(scores - log_total)
        probs_low = lax.optimization_barrier(probs.astype(jnp.bfloat16)).astype(jnp.float32)
        attended = lax.optimization_barrier(jnp.einsum('hqk,khd->qhd', probs_low, vals_all).astype(jnp.bfloat16)).astype(jnp.float32)
        delta = lax.optimization_barrier(jnp.sum(grad_block * attended, axis=2))
        dprob = jnp.einsum('qhd,khd->hqk', grad_block, vals_all)
        dscore = probs * (dprob - jnp.transpose(delta)[:, :, None]) * factor
        dscore = lax.optimization_barrier(dscore.astype(jnp.bfloat16)).astype(jnp.float32)
        grad_query = jnp.einsum('hqk,khd->qhd', dscore, keys_all).reshape(TILE, D)
        key_part = jnp.einsum('hqk,qhd->khd', dscore, query_block).reshape(-1, D)
        value_part = jnp.einsum('hqk,qhd->khd', probs_low, grad_block).reshape(-1, D)
        all_rows = jnp.concatenate([window_rows, global_ids.astype(jnp.int32)])
        return ((key_acc.at[all_rows].add(key_part), value_acc.at[all_rows].add(value_part)), grad_query)
    zero_grads = jnp.zeros((TOKENS, D), jnp.float32)
    (key_acc, value_acc), grad_tiles = lax.scan(one_tile, (zero_grads, zero_grads), jnp.arange(NT, dtype=jnp.int32))
    grad_qnorm = grad_tiles.reshape(TOKENS, D)
    query_grad = norm_grad(query_float, query_inv, grad_qnorm * query_gain)
    key_grad = norm_grad(key_float, key_inv, key_acc * key_gain)
    return (query_grad, key_grad, value_acc.astype(jnp.bfloat16))
```

```python
import functools

import jax
import jax.numpy as jnp
from jax import lax
from jax.experimental import pallas as pl
from jax.experimental.pallas import tpu as pltpu
from jax.sharding import PartitionSpec as P

HEAD_DIM = 128
D = 5120
TILE = 128
KEYS = 4
G_DEV = 2
MESH = pl.DeviceIdType.MESH

LOW = 8
ZN = 2

EPSILON = 1e-06


def normalize(as_float, gain, squares):
    inverse = lax.rsqrt(squares[:, None] / D + EPSILON)
    return (inverse, (as_float * inverse * gain).astype(jnp.bfloat16))


def norm_grad(as_float, inverse, scaled, coeffs):
    return (inverse * scaled - as_float * inverse**3 * (coeffs[:, None] / D)).astype(jnp.bfloat16)


def greet(targets):
    barrier = pltpu.get_barrier_semaphore()
    for target in targets:
        pl.semaphore_signal(barrier, inc=1, device_id=target, device_id_type=MESH)
    pl.semaphore_wait(barrier, len(targets))


def head_sum_kernel(count, x_ref, o_ref, slots, send_sem, recv_sem):
    me = lax.axis_index("head")
    peers = [{"head": lax.rem(me + o, count)} for o in range(1, count)]
    greet(peers)
    copies = []
    for o, peer in enumerate(peers):
        copy = pltpu.make_async_remote_copy(
            src_ref=x_ref,
            dst_ref=slots.at[o],
            send_sem=send_sem.at[o],
            recv_sem=recv_sem.at[o],
            device_id=peer,
            device_id_type=MESH,
        )
        copy.start()
        copies.append(copy)
    total = x_ref[...]
    for o, copy in enumerate(copies):
        copy.wait_recv()
        total = total + slots[o]
    o_ref[...] = total
    for copy in copies:
        copy.wait_send()


def head_sum(pair, collective_id):
    count = lax.axis_size("head")
    flat = pair.reshape(-1, 128)
    out = pl.pallas_call(
        functools.partial(head_sum_kernel, count),
        out_shape=jax.ShapeDtypeStruct(flat.shape, jnp.float32),
        in_specs=[pl.BlockSpec(memory_space=pltpu.VMEM)],
        out_specs=pl.BlockSpec(memory_space=pltpu.VMEM),
        scratch_shapes=[
            pltpu.VMEM((count - 1,) + flat.shape, jnp.float32),
            pltpu.SemaphoreType.DMA((count - 1,)),
            pltpu.SemaphoreType.DMA((count - 1,)),
        ],
        compiler_params=pltpu.CompilerParams(collective_id=collective_id, has_side_effects=True),
    )(flat)
    return out.reshape(pair.shape)


def places(count):
    me = lax.axis_index("ctx")
    yn = count // (LOW * ZN)
    low = lax.rem(me, LOW)
    z = lax.rem(me // LOW, ZN)
    y = me // (LOW * ZN)

    def at(y, z, low):
        return {"ctx": (y * ZN + z) * LOW + low}

    other_z = at(y, 1 - z, low)
    y_peers = [at(lax.rem(y + o, yn), z, low) for o in range(1, yn)]
    low_peers = [at(y, z, lax.rem(low + o, LOW)) for o in range(1, LOW)]
    after = {"ctx": lax.rem(me + 1, count)}
    before = {"ctx": lax.rem(me + count - 1, count)}
    return y, z, low, yn, other_z, y_peers, low_peers, after, before


def spread_kernel(count, kv_ref, own_ref, win_ref, glob_ref, wsend, wrecv, gsend, grecv, lsem):
    y, z, low, yn, other_z, y_peers, low_peers, after, before = places(count)
    greet([after, before, other_z] + y_peers + low_peers)

    def remote(src, dst, send_sem, recv_sem, target):
        return pltpu.make_async_remote_copy(
            src_ref=src,
            dst_ref=dst,
            send_sem=send_sem,
            recv_sem=recv_sem,
            device_id=target,
            device_id_type=MESH,
        )

    swap = remote(own_ref, glob_ref.at[low, y, z], gsend.at[0], grecv.at[0], other_z)
    swap.start()
    up = remote(kv_ref, win_ref.at[0], wsend.at[0], wrecv.at[0], after)
    down = remote(kv_ref, win_ref.at[1], wsend.at[1], wrecv.at[1], before)
    up.start()
    down.start()
    local = pltpu.make_async_copy(own_ref, glob_ref.at[low, y, z], lsem)
    local.start()
    local.wait()
    remote(own_ref, glob_ref.at[low, y, 1 - z], gsend.at[0], grecv.at[0], other_z).wait_recv()
    sent = [swap]
    for o, peer in enumerate(y_peers):
        copy = remote(glob_ref.at[low, y], glob_ref.at[low, y], gsend.at[1 + o], grecv.at[1 + o], peer)
        copy.start()
        sent.append(copy)
    for o, peer in enumerate(y_peers):
        source = lax.rem(y + yn - 1 - o, yn)
        remote(
            glob_ref.at[low, source], glob_ref.at[low, source], gsend.at[1 + o], grecv.at[1 + o], peer
        ).wait_recv()
    for o, peer in enumerate(low_peers):
        copy = remote(glob_ref.at[low], glob_ref.at[low], gsend.at[yn + o], grecv.at[yn + o], peer)
        copy.start()
        sent.append(copy)
    for o, peer in enumerate(low_peers):
        source = lax.rem(low + LOW - 1 - o, LOW)
        remote(
            glob_ref.at[source], glob_ref.at[source], gsend.at[yn + o], grecv.at[yn + o], peer
        ).wait_recv()
    up.wait()
    down.wait()
    for copy in sent:
        copy.wait_send()


def spread(key_value, own_rows):
    count = lax.axis_size("ctx")
    yn = count // (LOW * ZN)
    width = own_rows.shape[-1]
    copies = yn + LOW - 1
    return pl.pallas_call(
        functools.partial(spread_kernel, count),
        out_shape=(
            jax.ShapeDtypeStruct((2,) + key_value.shape, jnp.bfloat16),
            jax.ShapeDtypeStruct((LOW, yn, ZN, 2 * G_DEV, width), jnp.bfloat16),
        ),
        in_specs=[pl.BlockSpec(memory_space=pl.ANY)] * 2,
        out_specs=(pl.BlockSpec(memory_space=pl.ANY),) * 2,
        scratch_shapes=[
            pltpu.SemaphoreType.DMA((2,)),
            pltpu.SemaphoreType.DMA((2,)),
            pltpu.SemaphoreType.DMA((copies,)),
            pltpu.SemaphoreType.DMA((copies,)),
            pltpu.SemaphoreType.DMA,
        ],
        compiler_params=pltpu.CompilerParams(collective_id=1, has_side_effects=True),
    )(key_value, own_rows)


def collect_kernel(
    count, prev_ref, next_ref, part_ref, from_ref, sum_ref,
    slots, half, yslots, quarter, zslot, wsend, wrecv, gsend, grecv,
):
    y, z, low, yn, other_z, y_peers, low_peers, after, before = places(count)
    greet([after, before, other_z] + y_peers + low_peers)

    def remote(src, dst, send_sem, recv_sem, target):
        return pltpu.make_async_remote_copy(
            src_ref=src,
            dst_ref=dst,
            send_sem=send_sem,
            recv_sem=recv_sem,
            device_id=target,
            device_id_type=MESH,
        )

    sent = []
    for o, peer in enumerate(low_peers):
        copy = remote(
            part_ref.at[lax.rem(low + 1 + o, LOW)], slots.at[o], gsend.at[o], grecv.at[o], peer
        )
        copy.start()
        sent.append(copy)
    up = remote(next_ref, from_ref.at[0], wsend.at[0], wrecv.at[0], after)
    down = remote(prev_ref, from_ref.at[1], wsend.at[1], wrecv.at[1], before)
    up.start()
    down.start()
    total = part_ref[low]
    for o, copy in enumerate(sent):
        copy.wait_recv()
        total = total + slots[o]
    half[...] = total
    ysent = []
    for o, peer in enumerate(y_peers):
        index = LOW - 1 + o
        copy = remote(
            half.at[lax.rem(y + 1 + o, yn)], yslots.at[o], gsend.at[index], grecv.at[index], peer
        )
        copy.start()
        ysent.append(copy)
    row = half[y]
    for o, copy in enumerate(ysent):
        copy.wait_recv()
        row = row + yslots[o]
    quarter[...] = row
    last = LOW - 1 + yn - 1
    swap = remote(quarter, zslot, gsend.at[last], grecv.at[last], other_z)
    swap.start()
    swap.wait_recv()
    sum_ref[...] = row + zslot[...]
    for copy in sent + ysent + [swap]:
        copy.wait_send()
    up.wait()
    down.wait()


def collect(to_prev, to_next, parts):
    count = lax.axis_size("ctx")
    yn = count // (LOW * ZN)
    rows, width = parts.shape[2:]
    copies = LOW - 1 + yn
    return pl.pallas_call(
        functools.partial(collect_kernel, count),
        out_shape=(
            jax.ShapeDtypeStruct((2,) + to_prev.shape, jnp.bfloat16),
            jax.ShapeDtypeStruct((rows, width), jnp.float32),
        ),
        in_specs=[
            pl.BlockSpec(memory_space=pl.ANY),
            pl.BlockSpec(memory_space=pl.ANY),
            pl.BlockSpec(memory_space=pltpu.VMEM),
        ],
        out_specs=(pl.BlockSpec(memory_space=pl.ANY), pl.BlockSpec(memory_space=pltpu.VMEM)),
        scratch_shapes=[
            pltpu.VMEM((LOW - 1, yn, rows, width), jnp.float32),
            pltpu.VMEM((yn, rows, width), jnp.float32),
            pltpu.VMEM((yn - 1, rows, width), jnp.float32),
            pltpu.VMEM((rows, width), jnp.float32),
            pltpu.VMEM((rows, width), jnp.float32),
            pltpu.SemaphoreType.DMA((2,)),
            pltpu.SemaphoreType.DMA((2,)),
            pltpu.SemaphoreType.DMA((copies,)),
            pltpu.SemaphoreType.DMA((copies,)),
        ],
        compiler_params=pltpu.CompilerParams(collective_id=2, has_side_effects=True),
    )(to_prev, to_next, parts)


def dot(a, b, dims):
    return lax.dot_general(a, b, (dims, ((), ())), preferred_element_type=jnp.float32)


ROWS = ((1,), (0,))
TURNED = ((1,), (1,))
DOWN = ((0,), (0,))


def attention_kernel(
    start_ref, live_ref, q_ref, g_ref, kv_ref, win_ref, glob_ref,
    dq_ref, prev_ref, next_ref, own_ref, dglob_ref, keys, vals, dkeys, dvals,
):
    tokens = q_ref.shape[0]
    span = KEYS * TILE
    factor = HEAD_DIM ** (-0.5)
    for pair_index, cat in enumerate((keys, vals)):
        cat[0:tokens] = win_ref[0, pair_index]
        cat[tokens : 2 * tokens] = kv_ref[pair_index]
        cat[2 * tokens :] = win_ref[1, pair_index]
    dkeys[...] = jnp.zeros_like(dkeys)
    dvals[...] = jnp.zeros_like(dvals)
    gkeys = glob_ref[0]
    gvals = glob_ref[1]
    live = live_ref[...] > 0
    gdk = 0.0
    gdv = 0.0
    for tile in range(tokens // TILE):
        rows = slice(tile * TILE, (tile + 1) * TILE)
        window = pl.ds(pl.multiple_of(start_ref[tile] * TILE, TILE), span)
        query = q_ref[rows]
        grad = g_ref[rows]
        wkeys = keys[window]
        wvals = vals[window]
        score_w = dot(query, wkeys, TURNED) * factor
        score_g = jnp.where(live, dot(query, gkeys, TURNED) * factor, -jnp.inf)
        largest = jnp.maximum(
            jnp.max(score_w, axis=1, keepdims=True), jnp.max(score_g, axis=1, keepdims=True)
        )
        exp_w = jnp.exp(score_w - largest)
        exp_g = jnp.exp(score_g - largest)
        inverse = 1.0 / (
            jnp.sum(exp_w, axis=1, keepdims=True) + jnp.sum(exp_g, axis=1, keepdims=True)
        )
        prob_w = exp_w * inverse
        prob_g = exp_g * inverse
        low_w = prob_w.astype(jnp.bfloat16)
        low_g = prob_g.astype(jnp.bfloat16)
        attended = (dot(low_w, wvals, ROWS) + dot(low_g, gvals, ROWS)).astype(jnp.bfloat16)
        delta = jnp.sum(
            grad.astype(jnp.float32) * attended.astype(jnp.float32), axis=1, keepdims=True
        )
        ds_w = (prob_w * (dot(grad, wvals, TURNED) - delta) * factor).astype(jnp.bfloat16)
        ds_g = (prob_g * (dot(grad, gvals, TURNED) - delta) * factor).astype(jnp.bfloat16)
        dq_ref[rows] = dot(ds_w, wkeys, ROWS) + dot(ds_g, gkeys, ROWS)
        dkeys[window] += dot(ds_w, query, DOWN)
        dvals[window] += dot(low_w, grad, DOWN)
        gdk = gdk + dot(ds_g, query, DOWN)
        gdv = gdv + dot(low_g, grad, DOWN)
    for pair_index, cat in enumerate((dkeys, dvals)):
        prev_ref[pair_index] = cat[0:tokens].astype(jnp.bfloat16)
        own_ref[pair_index] = cat[tokens : 2 * tokens]
        next_ref[pair_index] = cat[2 * tokens :].astype(jnp.bfloat16)
    dglob_ref[0] = gdk
    dglob_ref[1] = gdv


def attention(starts, live, query_norm, out_grad, key_value, window, globs):
    tokens, width = query_norm.shape
    count = globs.shape[1]
    flat = pl.BlockSpec((tokens, HEAD_DIM), lambda h: (0, h))
    pair = pl.BlockSpec((2, tokens, HEAD_DIM), lambda h: (0, 0, h))
    glob = pl.BlockSpec((2, count, HEAD_DIM), lambda h: (0, 0, h))
    pair_shape = (2, tokens, width)
    return pl.pallas_call(
        attention_kernel,
        grid=(width // HEAD_DIM,),
        out_shape=(
            jax.ShapeDtypeStruct((tokens, width), jnp.float32),
            jax.ShapeDtypeStruct(pair_shape, jnp.bfloat16),
            jax.ShapeDtypeStruct(pair_shape, jnp.bfloat16),
            jax.ShapeDtypeStruct(pair_shape, jnp.float32),
            jax.ShapeDtypeStruct((2, count, width), jnp.float32),
        ),
        in_specs=[
            pl.BlockSpec(memory_space=pltpu.SMEM),
            pl.BlockSpec(memory_space=pltpu.VMEM),
            flat,
            flat,
            pair,
            pl.BlockSpec((2, 2, tokens, HEAD_DIM), lambda h: (0, 0, 0, h)),
            glob,
        ],
        out_specs=(flat, pair, pair, pair, glob),
        scratch_shapes=[
            pltpu.VMEM((3 * tokens, HEAD_DIM), jnp.bfloat16),
            pltpu.VMEM((3 * tokens, HEAD_DIM), jnp.bfloat16),
            pltpu.VMEM((3 * tokens, HEAD_DIM), jnp.float32),
            pltpu.VMEM((3 * tokens, HEAD_DIM), jnp.float32),
        ],
    )(starts, live, query_norm, out_grad, key_value, window, globs)


def body(
    query_raw, key_raw, values, out_grad, query_gain, key_gain, key_tiles, global_ids, readers
):
    tokens_here, width = query_raw.shape
    tiles_here = tokens_here // TILE
    count = lax.axis_size("ctx")
    yn = count // (LOW * ZN)
    device = lax.axis_index("ctx")
    query_rows = query_raw.astype(jnp.float32)
    key_rows = key_raw.astype(jnp.float32)
    squares = head_sum(
        jnp.stack([jnp.sum(query_rows * query_rows, axis=1), jnp.sum(key_rows * key_rows, axis=1)]),
        0,
    )
    query_inv, query_norm = normalize(query_rows, query_gain, squares[0])
    key_inv, key_norm = normalize(key_rows, key_gain, squares[1])
    key_value = jnp.stack([key_norm, values])
    own_rows = global_ids - device * tokens_here
    own_pair = key_value[:, own_rows].reshape(2 * G_DEV, width)
    window, globs = spread(key_value, own_pair)
    globs = (
        globs.reshape(LOW, yn, ZN, 2, G_DEV, width)
        .transpose(3, 1, 2, 0, 4, 5)
        .reshape(2, count * G_DEV, width)
    )
    live = jnp.repeat(readers, G_DEV, axis=1)
    starts = jnp.clip(key_tiles[:, 0] - (device - 1) * tiles_here, 0, 3 * tiles_here - KEYS)
    grad_query, to_prev, to_next, own_grads, glob_grads = attention(
        starts, live, query_norm, out_grad, key_value, window, globs
    )
    parts = (
        glob_grads.reshape(2, yn, ZN, LOW, G_DEV, width)
        .transpose(3, 1, 2, 0, 4, 5)
        .reshape(LOW, yn, ZN * 2 * G_DEV, width)
    )
    arrived, reduced = collect(to_prev, to_next, parts)
    mine = lax.dynamic_index_in_dim(
        reduced.reshape(ZN, 2, G_DEV, width), lax.rem(device // LOW, ZN), 0, keepdims=False
    )
    home = own_grads + arrived[0].astype(jnp.float32) + arrived[1].astype(jnp.float32)
    spots = jnp.arange(tokens_here, dtype=jnp.int32)[:, None]
    for index in range(G_DEV):
        home = home + jnp.where(spots == own_rows[index], mine[:, index][:, None, :], 0.0)
    scaled_query = grad_query * query_gain
    scaled_key = home[0] * key_gain
    dots = head_sum(
        jnp.stack([jnp.sum(scaled_query * query_rows, axis=1), jnp.sum(scaled_key * key_rows, axis=1)]),
        3,
    )
    query_grad = norm_grad(query_rows, query_inv, scaled_query, dots[0])
    key_grad = norm_grad(key_rows, key_inv, scaled_key, dots[1])
    return (query_grad, key_grad, home[1].astype(jnp.bfloat16))


def solution(mesh):
    return jax.shard_map(
        body,
        mesh=mesh,
        in_specs=(
            P("ctx", "head"),
            P("ctx", "head"),
            P("ctx", "head"),
            P("ctx", "head"),
            P("head"),
            P("head"),
            P("ctx", None),
            P("ctx"),
            P("ctx", None),
        ),
        out_specs=(P("ctx", "head"), P("ctx", "head"), P("ctx", "head")),
        check_vma=False,
    )
```

```python
import functools

import jax
import jax.numpy as jnp
from jax import lax
from jax.experimental import pallas as pl
from jax.experimental.pallas import tpu as pltpu
from jax.sharding import PartitionSpec as P

HEAD_DIM = 128
D = 5120
TILE = 128
KEYS = 4
G_DEV = 2
MESH = pl.DeviceIdType.MESH

LOW = 8
ZN = 2

EPSILON = 1e-06


def norm_grad(as_float, inverse, scaled, coeffs):
    return (inverse * scaled - as_float * inverse**3 * (coeffs[:, None] / D)).astype(jnp.bfloat16)


def greet(targets):
    barrier = pltpu.get_barrier_semaphore()
    for target in targets:
        pl.semaphore_signal(barrier, inc=1, device_id=target, device_id_type=MESH)
    pl.semaphore_wait(barrier, len(targets))


def remote(src, dst, sems, index, target):
    return pltpu.make_async_remote_copy(
        src_ref=src,
        dst_ref=dst,
        send_sem=sems[0].at[index],
        recv_sem=sems[1].at[index],
        device_id=target,
        device_id_type=MESH,
    )


def head_peers(heads):
    me = lax.axis_index("head")
    return [{"head": lax.rem(me + o, heads)} for o in range(1, heads)]


def start_all(src, slots, sems, peers):
    copies = [remote(src, slots.at[o], sems, o, peer) for o, peer in enumerate(peers)]
    for copy in copies:
        copy.start()
    return copies


def add_arrivals(total, slots, copies):
    for o, copy in enumerate(copies):
        copy.wait_recv()
        total = total + slots[o]
    return total


def places(count):
    me = lax.axis_index("ctx")
    yn = count // (LOW * ZN)
    low = lax.rem(me, LOW)
    z = lax.rem(me // LOW, ZN)
    y = me // (LOW * ZN)

    def at(y, z, low):
        return {"ctx": (y * ZN + z) * LOW + low}

    other_z = at(y, 1 - z, low)
    y_peers = [at(lax.rem(y + o, yn), z, low) for o in range(1, yn)]
    low_peers = [at(y, z, lax.rem(low + o, LOW)) for o in range(1, LOW)]
    after = {"ctx": lax.rem(me + 1, count)}
    before = {"ctx": lax.rem(me + count - 1, count)}
    return y, z, low, yn, other_z, y_peers, low_peers, after, before


def spread_kernel(
    count, heads, key_ref, val_ref, sq_ref, raw_ref, gain_ref,
    win_ref, glob_ref, tot_ref, near_ref,
    hslots, total_buf, near_buf, own_buf, wsend, wrecv, hsend, hrecv, gsend, grecv, lsem,
):
    y, z, low, yn, other_z, y_peers, low_peers, after, before = places(count)
    peers = head_peers(heads)
    greet(peers + [after, before, other_z] + y_peers + low_peers)
    wsems, hsems, gsems = (wsend, wrecv), (hsend, hrecv), (gsend, grecv)
    summed = start_all(sq_ref, hslots, hsems, peers)
    moved = [
        remote(key_ref, win_ref.at[0, 0], wsems, 0, after),
        remote(key_ref, win_ref.at[1, 0], wsems, 1, before),
    ]
    for copy in moved:
        copy.start()
    total = add_arrivals(sq_ref[...], hslots, summed)
    total_buf[...] = total
    tot_ref[...] = total
    raw = raw_ref[...]
    inverse = lax.rsqrt(total[4:8, 0:1] / D + EPSILON)
    is_key = lax.broadcasted_iota(jnp.int32, raw.shape, 0) < G_DEV
    own_buf[...] = jnp.where(is_key, raw * inverse * gain_ref[...], raw).astype(jnp.bfloat16)
    swap = remote(own_buf, glob_ref.at[low, y, z], gsems, 0, other_z)
    swap.start()
    local = pltpu.make_async_copy(own_buf, glob_ref.at[low, y, z], lsem)
    local.start()
    near = [
        remote(total_buf, near_buf.at[0], wsems, 4, after),
        remote(total_buf, near_buf.at[1], wsems, 5, before),
    ]
    for copy in near:
        copy.start()
    local.wait()
    remote(own_buf, glob_ref.at[low, y, 1 - z], gsems, 0, other_z).wait_recv()
    sent = [swap]
    for o, peer in enumerate(y_peers):
        copy = remote(glob_ref.at[low, y], glob_ref.at[low, y], gsems, 1 + o, peer)
        copy.start()
        sent.append(copy)
    for o, peer in enumerate(y_peers):
        source = lax.rem(y + yn - 1 - o, yn)
        remote(glob_ref.at[low, source], glob_ref.at[low, source], gsems, 1 + o, peer).wait_recv()
    for o, peer in enumerate(low_peers):
        copy = remote(glob_ref.at[low], glob_ref.at[low], gsems, yn + o, peer)
        copy.start()
        sent.append(copy)
    late = [
        remote(val_ref, win_ref.at[0, 1], wsems, 2, after),
        remote(val_ref, win_ref.at[1, 1], wsems, 3, before),
    ]
    for copy in late:
        copy.start()
    for o, peer in enumerate(low_peers):
        source = lax.rem(low + LOW - 1 - o, LOW)
        remote(glob_ref.at[source], glob_ref.at[source], gsems, yn + o, peer).wait_recv()
    for copy in near:
        copy.wait()
    near_ref[...] = near_buf[...]
    for copy in moved + late:
        copy.wait()
    for copy in sent + summed:
        copy.wait_send()


def spread(key_raw, values, squares, own_raw, gain):
    count = lax.axis_size("ctx")
    heads = lax.axis_size("head")
    yn = count // (LOW * ZN)
    width = own_raw.shape[-1]
    copies = yn + LOW - 1
    vmem = pl.BlockSpec(memory_space=pltpu.VMEM)
    free = pl.BlockSpec(memory_space=pl.ANY)
    return pl.pallas_call(
        functools.partial(spread_kernel, count, heads),
        out_shape=(
            jax.ShapeDtypeStruct((2, 2) + key_raw.shape, jnp.bfloat16),
            jax.ShapeDtypeStruct((LOW, yn, ZN, 2 * G_DEV, width), jnp.bfloat16),
            jax.ShapeDtypeStruct(squares.shape, jnp.float32),
            jax.ShapeDtypeStruct((2,) + squares.shape, jnp.float32),
        ),
        in_specs=[free, free, vmem, vmem, vmem],
        out_specs=(free, free, vmem, vmem),
        scratch_shapes=[
            pltpu.VMEM((heads - 1,) + squares.shape, jnp.float32),
            pltpu.VMEM(squares.shape, jnp.float32),
            pltpu.VMEM((2,) + squares.shape, jnp.float32),
            pltpu.VMEM(own_raw.shape, jnp.bfloat16),
            pltpu.SemaphoreType.DMA((6,)),
            pltpu.SemaphoreType.DMA((6,)),
            pltpu.SemaphoreType.DMA((heads - 1,)),
            pltpu.SemaphoreType.DMA((heads - 1,)),
            pltpu.SemaphoreType.DMA((copies,)),
            pltpu.SemaphoreType.DMA((copies,)),
            pltpu.SemaphoreType.DMA,
        ],
        compiler_params=pltpu.CompilerParams(collective_id=1, has_side_effects=True),
    )(key_raw, values, squares, own_raw, gain)


def collect_kernel(
    count, heads, prev_ref, next_ref, part_ref, dots_ref, weight_ref,
    from_ref, sum_ref, tot_ref, near_ref, extra_ref,
    slots, half, yslots, quarter, zslot, hslots, total_buf, near_buf, extra_buf, eslots,
    wsend, wrecv, gsend, grecv, hsend, hrecv, esend, erecv,
):
    y, z, low, yn, other_z, y_peers, low_peers, after, before = places(count)
    peers = head_peers(heads)
    greet(peers + [after, before, other_z] + y_peers + low_peers)
    wsems, hsems, gsems, esems = (wsend, wrecv), (hsend, hrecv), (gsend, grecv), (esend, erecv)
    dotted = start_all(dots_ref, hslots, hsems, peers)
    sent = []
    for o, peer in enumerate(low_peers):
        copy = remote(part_ref.at[lax.rem(low + 1 + o, LOW)], slots.at[o], gsems, o, peer)
        copy.start()
        sent.append(copy)
    moved = [
        remote(next_ref, from_ref.at[0], wsems, 0, after),
        remote(prev_ref, from_ref.at[1], wsems, 1, before),
    ]
    for copy in moved:
        copy.start()
    total = add_arrivals(dots_ref[...], hslots, dotted)
    total_buf[...] = total
    tot_ref[...] = total
    near = [
        remote(total_buf, near_buf.at[0], wsems, 2, after),
        remote(total_buf, near_buf.at[1], wsems, 3, before),
    ]
    for copy in near:
        copy.start()
    half[...] = add_arrivals(part_ref[low], slots, sent)
    ysent = []
    for o, peer in enumerate(y_peers):
        copy = remote(half.at[lax.rem(y + 1 + o, yn)], yslots.at[o], gsems, LOW - 1 + o, peer)
        copy.start()
        ysent.append(copy)
    row = add_arrivals(half[y], yslots, ysent)
    quarter[...] = row
    swap = remote(quarter, zslot, gsems, LOW - 1 + yn - 1, other_z)
    swap.start()
    swap.wait_recv()
    reduced = row + zslot[...]
    sum_ref[...] = reduced
    share = jnp.sum(reduced * weight_ref[...], axis=1, keepdims=True)
    extra = jnp.broadcast_to(share, extra_buf.shape)
    extra_buf[...] = extra
    extras = start_all(extra_buf, eslots, esems, peers)
    extra_ref[...] = add_arrivals(extra, eslots, extras)
    for copy in near:
        copy.wait()
    near_ref[...] = near_buf[...]
    for copy in moved:
        copy.wait()
    for copy in sent + ysent + [swap] + dotted + extras:
        copy.wait_send()


def collect(to_prev, to_next, parts, dots, weight):
    count = lax.axis_size("ctx")
    heads = lax.axis_size("head")
    yn = count // (LOW * ZN)
    rows, width = parts.shape[2:]
    copies = LOW - 1 + yn
    vmem = pl.BlockSpec(memory_space=pltpu.VMEM)
    free = pl.BlockSpec(memory_space=pl.ANY)
    return pl.pallas_call(
        functools.partial(collect_kernel, count, heads),
        out_shape=(
            jax.ShapeDtypeStruct((2,) + to_prev.shape, jnp.bfloat16),
            jax.ShapeDtypeStruct((rows, width), jnp.float32),
            jax.ShapeDtypeStruct(dots.shape, jnp.float32),
            jax.ShapeDtypeStruct((2,) + dots.shape, jnp.float32),
            jax.ShapeDtypeStruct((rows, 128), jnp.float32),
        ),
        in_specs=[free, free, vmem, vmem, vmem],
        out_specs=(free, vmem, vmem, vmem, vmem),
        scratch_shapes=[
            pltpu.VMEM((LOW - 1, yn, rows, width), jnp.float32),
            pltpu.VMEM((yn, rows, width), jnp.float32),
            pltpu.VMEM((yn - 1, rows, width), jnp.float32),
            pltpu.VMEM((rows, width), jnp.float32),
            pltpu.VMEM((rows, width), jnp.float32),
            pltpu.VMEM((heads - 1,) + dots.shape, jnp.float32),
            pltpu.VMEM(dots.shape, jnp.float32),
            pltpu.VMEM((2,) + dots.shape, jnp.float32),
            pltpu.VMEM((rows, 128), jnp.float32),
            pltpu.VMEM((heads - 1, rows, 128), jnp.float32),
            pltpu.SemaphoreType.DMA((4,)),
            pltpu.SemaphoreType.DMA((4,)),
            pltpu.SemaphoreType.DMA((copies,)),
            pltpu.SemaphoreType.DMA((copies,)),
            pltpu.SemaphoreType.DMA((heads - 1,)),
            pltpu.SemaphoreType.DMA((heads - 1,)),
            pltpu.SemaphoreType.DMA((heads - 1,)),
            pltpu.SemaphoreType.DMA((heads - 1,)),
        ],
        compiler_params=pltpu.CompilerParams(collective_id=2, has_side_effects=True),
    )(to_prev, to_next, parts, dots, weight)


def dot(a, b, dims):
    return lax.dot_general(a, b, (dims, ((), ())), preferred_element_type=jnp.float32)


ROWS = ((1,), (0,))
TURNED = ((1,), (1,))
DOWN = ((0,), (0,))


def attention_kernel(
    start_ref, live_ref, tot_ref, near_ref, qgain_ref, kgain_ref,
    q_ref, g_ref, key_ref, val_ref, win_ref, glob_ref,
    dq_ref, prev_ref, next_ref, own_ref, dglob_ref, dots_ref,
    inverses, queries, keys, vals, dkeys, dvals, dot_sums,
):
    tokens = q_ref.shape[0]
    span = KEYS * TILE
    factor = HEAD_DIM ** (-0.5)

    @pl.when(pl.program_id(0) == 0)
    def _():
        own = lax.rsqrt(tot_ref[...] / D + EPSILON)
        near = lax.rsqrt(near_ref[...] / D + EPSILON)
        lines = [own[0:1], own[1:2], near[0, 2:3], near[0, 3:4]]
        lines += [own[2:3], own[3:4], near[1, 2:3], near[1, 3:4]]
        for index, line in enumerate(lines):
            inverses[index * TILE : (index + 1) * TILE] = jnp.broadcast_to(line, (TILE, TILE)).T
        dot_sums[...] = jnp.zeros_like(dot_sums)

    qgain = qgain_ref[...]
    kgain = kgain_ref[...]
    query_rows = q_ref[...].astype(jnp.float32)
    queries[...] = (query_rows * inverses[0:tokens] * qgain).astype(jnp.bfloat16)
    blocks = [win_ref[0, 0], key_ref[...], win_ref[1, 0]]
    for index, block in enumerate(blocks):
        rows = slice(index * tokens, (index + 1) * tokens)
        scale = inverses[(index + 1) * tokens : (index + 2) * tokens]
        keys[rows] = (block.astype(jnp.float32) * scale * kgain).astype(jnp.bfloat16)
    vals[0:tokens] = win_ref[0, 1]
    vals[tokens : 2 * tokens] = val_ref[...]
    vals[2 * tokens :] = win_ref[1, 1]
    dkeys[...] = jnp.zeros_like(dkeys)
    dvals[...] = jnp.zeros_like(dvals)
    gkeys = glob_ref[0]
    gvals = glob_ref[1]
    live = live_ref[...] > 0
    gdk = 0.0
    gdv = 0.0
    for tile in range(tokens // TILE):
        rows = slice(tile * TILE, (tile + 1) * TILE)
        window = pl.ds(pl.multiple_of(start_ref[tile] * TILE, TILE), span)
        query = queries[rows]
        grad = g_ref[rows]
        wkeys = keys[window]
        wvals = vals[window]
        score_w = dot(query, wkeys, TURNED) * factor
        score_g = jnp.where(live, dot(query, gkeys, TURNED) * factor, -jnp.inf)
        largest = jnp.maximum(
            jnp.max(score_w, axis=1, keepdims=True), jnp.max(score_g, axis=1, keepdims=True)
        )
        exp_w = jnp.exp(score_w - largest)
        exp_g = jnp.exp(score_g - largest)
        inverse = 1.0 / (
            jnp.sum(exp_w, axis=1, keepdims=True) + jnp.sum(exp_g, axis=1, keepdims=True)
        )
        prob_w = exp_w * inverse
        prob_g = exp_g * inverse
        low_w = prob_w.astype(jnp.bfloat16)
        low_g = prob_g.astype(jnp.bfloat16)
        attended = (dot(low_w, wvals, ROWS) + dot(low_g, gvals, ROWS)).astype(jnp.bfloat16)
        delta = jnp.sum(
            grad.astype(jnp.float32) * attended.astype(jnp.float32), axis=1, keepdims=True
        )
        ds_w = (prob_w * (dot(grad, wvals, TURNED) - delta) * factor).astype(jnp.bfloat16)
        ds_g = (prob_g * (dot(grad, gvals, TURNED) - delta) * factor).astype(jnp.bfloat16)
        dq_ref[rows] = dot(ds_w, wkeys, ROWS) + dot(ds_g, gkeys, ROWS)
        dkeys[window] += dot(ds_w, query, DOWN)
        dvals[window] += dot(low_w, grad, DOWN)
        gdk = gdk + dot(ds_g, query, DOWN)
        gdv = gdv + dot(low_g, grad, DOWN)
    for pair_index, cat in enumerate((dkeys, dvals)):
        prev_ref[pair_index] = cat[0:tokens].astype(jnp.bfloat16)
        own_ref[pair_index] = cat[tokens : 2 * tokens]
        next_ref[pair_index] = cat[2 * tokens :].astype(jnp.bfloat16)
    dglob_ref[0] = gdk
    dglob_ref[1] = gdv
    dot_sums[0:tokens] += dq_ref[...] * qgain * query_rows
    for index, block in enumerate(blocks):
        rows = slice(index * tokens, (index + 1) * tokens)
        dot_sums[(index + 1) * tokens : (index + 2) * tokens] += (
            dkeys[rows] * kgain * block.astype(jnp.float32)
        )

    @pl.when(pl.program_id(0) == pl.num_programs(0) - 1)
    def _():
        for index in range(dots_ref.shape[0]):
            turned = dot_sums[index * TILE : (index + 1) * TILE].T
            dots_ref[index : index + 1] = jnp.sum(turned, axis=0, keepdims=True)


def attention(starts, live, totals, near, qgain, kgain, query, out_grad, key, val, window, globs):
    tokens, width = query.shape
    count = globs.shape[1]
    whole = pl.BlockSpec(memory_space=pltpu.VMEM)
    flat = pl.BlockSpec((tokens, HEAD_DIM), lambda h: (0, h))
    gain = pl.BlockSpec((1, HEAD_DIM), lambda h: (0, h))
    pair = pl.BlockSpec((2, tokens, HEAD_DIM), lambda h: (0, 0, h))
    glob = pl.BlockSpec((2, count, HEAD_DIM), lambda h: (0, 0, h))
    pair_shape = (2, tokens, width)
    lines = 4 * tokens // TILE
    return pl.pallas_call(
        attention_kernel,
        grid=(width // HEAD_DIM,),
        out_shape=(
            jax.ShapeDtypeStruct((tokens, width), jnp.float32),
            jax.ShapeDtypeStruct(pair_shape, jnp.bfloat16),
            jax.ShapeDtypeStruct(pair_shape, jnp.bfloat16),
            jax.ShapeDtypeStruct(pair_shape, jnp.float32),
            jax.ShapeDtypeStruct((2, count, width), jnp.float32),
            jax.ShapeDtypeStruct((lines, TILE), jnp.float32),
        ),
        in_specs=[
            pl.BlockSpec(memory_space=pltpu.SMEM),
            whole,
            whole,
            whole,
            gain,
            gain,
            flat,
            flat,
            flat,
            flat,
            pl.BlockSpec((2, 2, tokens, HEAD_DIM), lambda h: (0, 0, 0, h)),
            glob,
        ],
        out_specs=(flat, pair, pair, pair, glob, pl.BlockSpec((lines, TILE), lambda h: (0, 0))),
        scratch_shapes=[
            pltpu.VMEM((4 * tokens, HEAD_DIM), jnp.float32),
            pltpu.VMEM((tokens, HEAD_DIM), jnp.bfloat16),
            pltpu.VMEM((3 * tokens, HEAD_DIM), jnp.bfloat16),
            pltpu.VMEM((3 * tokens, HEAD_DIM), jnp.bfloat16),
            pltpu.VMEM((3 * tokens, HEAD_DIM), jnp.float32),
            pltpu.VMEM((3 * tokens, HEAD_DIM), jnp.float32),
            pltpu.VMEM((4 * tokens, HEAD_DIM), jnp.float32),
        ],
    )(starts, live, totals, near, qgain, kgain, query, out_grad, key, val, window, globs)


def body(
    query_raw, key_raw, values, out_grad, query_gain, key_gain, key_tiles, global_ids, readers
):
    tokens_here, width = query_raw.shape
    tiles_here = tokens_here // TILE
    count = lax.axis_size("ctx")
    yn = count // (LOW * ZN)
    device = lax.axis_index("ctx")
    query_rows = query_raw.astype(jnp.float32)
    key_rows = key_raw.astype(jnp.float32)
    own_rows = global_ids - device * tokens_here
    own_keys = key_raw[own_rows].astype(jnp.float32)
    own_vals = values[own_rows].astype(jnp.float32)
    own_squares = jnp.sum(own_keys * own_keys, axis=1)
    squares = jnp.concatenate(
        [
            jnp.sum(query_rows * query_rows, axis=1).reshape(tiles_here, TILE),
            jnp.sum(key_rows * key_rows, axis=1).reshape(tiles_here, TILE),
            jnp.broadcast_to(own_squares[:, None], (G_DEV, TILE)),
            jnp.zeros((G_DEV, TILE), jnp.float32),
        ]
    )
    qgain = query_gain[None, :]
    kgain = key_gain[None, :]
    window, globs, totals, near = spread(
        key_raw, values, squares, jnp.concatenate([own_keys, own_vals]), kgain
    )
    globs = (
        globs.reshape(LOW, yn, ZN, 2, G_DEV, width)
        .transpose(3, 1, 2, 0, 4, 5)
        .reshape(2, count * G_DEV, width)
    )
    live = jnp.repeat(readers, G_DEV, axis=1)
    starts = jnp.clip(key_tiles[:, 0] - (device - 1) * tiles_here, 0, 3 * tiles_here - KEYS)
    grad_query, to_prev, to_next, own_grads, glob_grads, dots = attention(
        starts, live, totals, near, qgain, kgain, query_raw, out_grad, key_raw, values, window, globs
    )
    parts = (
        glob_grads.reshape(2, yn, ZN, LOW, G_DEV, width)
        .transpose(3, 1, 2, 0, 4, 5)
        .reshape(LOW, yn, ZN * 2 * G_DEV, width)
    )
    z = lax.rem(device // LOW, ZN)
    weight = jnp.where(
        (jnp.arange(ZN)[:, None] == z)[:, :, None, None] & (jnp.arange(2) == 0)[None, :, None, None],
        (own_keys * key_gain)[None, None],
        0.0,
    ).reshape(ZN * 2 * G_DEV, width)
    arrived, reduced, dot_totals, dot_near, extra = collect(to_prev, to_next, parts, dots, weight)
    mine = lax.dynamic_index_in_dim(
        reduced.reshape(ZN, 2, G_DEV, width), z, 0, keepdims=False
    )
    extra = extra.reshape(ZN, 2, G_DEV, 128)[:, 0, :, 0].sum(axis=0)
    home = own_grads + arrived[0].astype(jnp.float32) + arrived[1].astype(jnp.float32)
    spots = jnp.arange(tokens_here, dtype=jnp.int32)
    query_dot = dot_totals[0:2].reshape(-1)
    key_dot = (dot_totals[4:6] + dot_near[0, 6:8] + dot_near[1, 2:4]).reshape(-1)
    for index in range(G_DEV):
        here = spots == own_rows[index]
        home = home + jnp.where(here[:, None], mine[:, index][:, None, :], 0.0)
        key_dot = key_dot + jnp.where(here, extra[index], 0.0)
    query_inv = lax.rsqrt(totals[0:2].reshape(-1, 1) / D + EPSILON)
    key_inv = lax.rsqrt(totals[2:4].reshape(-1, 1) / D + EPSILON)
    query_grad = norm_grad(query_rows, query_inv, grad_query * query_gain, query_dot)
    key_grad = norm_grad(key_rows, key_inv, home[0] * key_gain, key_dot)
    return (query_grad, key_grad, home[1].astype(jnp.bfloat16))


def solution(mesh):
    return jax.shard_map(
        body,
        mesh=mesh,
        in_specs=(
            P("ctx", "head"),
            P("ctx", "head"),
            P("ctx", "head"),
            P("ctx", "head"),
            P("head"),
            P("head"),
            P("ctx", None),
            P("ctx"),
            P("ctx", None),
        ),
        out_specs=(P("ctx", "head"), P("ctx", "head"), P("ctx", "head")),
        check_vma=False,
    )
```

```python
import functools

import jax
import jax.numpy as jnp
from jax import lax
from jax.experimental import pallas as pl
from jax.experimental.pallas import tpu as pltpu
from jax.sharding import PartitionSpec as P

HEAD_DIM = 128
D = 5120
TILE = 128
KEYS = 4
G_DEV = 2
MESH = pl.DeviceIdType.MESH

LOW = 8
ZN = 2

EPSILON = 1e-06


def dot(a, b, dims):
    return lax.dot_general(a, b, (dims, ((), ())), preferred_element_type=jnp.float32)


ROWS = ((1,), (0,))
TURNED = ((1,), (1,))
DOWN = ((0,), (0,))


def greet(targets):
    barrier = pltpu.get_barrier_semaphore()
    for target in targets:
        pl.semaphore_signal(barrier, inc=1, device_id=target, device_id_type=MESH)
    pl.semaphore_wait(barrier, len(targets))


def remote(src, dst, sems, index, target):
    return pltpu.make_async_remote_copy(
        src_ref=src,
        dst_ref=dst,
        send_sem=sems[0].at[index],
        recv_sem=sems[1].at[index],
        device_id=target,
        device_id_type=MESH,
    )


def head_peers(heads):
    me = lax.axis_index("head")
    return [{"head": lax.rem(me + o, heads)} for o in range(1, heads)]


def start_all(src, slots, sems, peers):
    copies = [remote(src, slots.at[o], sems, o, peer) for o, peer in enumerate(peers)]
    for copy in copies:
        copy.start()
    return copies


def add_arrivals(total, slots, copies):
    for o, copy in enumerate(copies):
        copy.wait_recv()
        total = total + slots[o]
    return total


def places(count):
    me = lax.axis_index("ctx")
    yn = count // (LOW * ZN)
    low = lax.rem(me, LOW)
    z = lax.rem(me // LOW, ZN)
    y = me // (LOW * ZN)

    def at(y, z, low):
        return {"ctx": (y * ZN + z) * LOW + low}

    other_z = at(y, 1 - z, low)
    y_peers = [at(lax.rem(y + o, yn), z, low) for o in range(1, yn)]
    low_peers = [at(y, z, lax.rem(low + o, LOW)) for o in range(1, LOW)]
    after = {"ctx": lax.rem(me + 1, count)}
    before = {"ctx": lax.rem(me + count - 1, count)}
    return y, z, low, yn, other_z, y_peers, low_peers, after, before


def own_tokens(ids_ref, first, key_ref, val_ref):
    tokens = key_ref.shape[0]
    rows = lax.broadcasted_iota(jnp.int32, (8, tokens), 0)
    spots = lax.broadcasted_iota(jnp.int32, (8, tokens), 1)
    picks = jnp.zeros((8, tokens), jnp.float32)
    for index in range(G_DEV):
        hit = (rows % G_DEV == index) & (spots == ids_ref[index] - first)
        picks = jnp.where(hit, 1.0, picks)
    picks = picks.astype(jnp.bfloat16)
    keys = dot(picks, key_ref[...], ROWS)[0:4]
    vals = dot(picks, val_ref[...], ROWS)[0:4]
    is_key = lax.broadcasted_iota(jnp.int32, keys.shape, 0) < G_DEV
    return jnp.where(is_key, keys, vals)


def spread_kernel(
    count, heads, ids_ref, query_ref, key_ref, val_ref, gain_ref,
    win_ref, glob_ref, tot_ref, near_ref,
    sq_buf, hslots, total_buf, near_buf, own_buf, wsend, wrecv, hsend, hrecv, gsend, grecv, lsem,
):
    y, z, low, yn, other_z, y_peers, low_peers, after, before = places(count)
    peers = head_peers(heads)
    greet(peers + [after, before, other_z] + y_peers + low_peers)
    wsems, hsems, gsems = (wsend, wrecv), (hsend, hrecv), (gsend, grecv)
    moved = [
        remote(key_ref, win_ref.at[0, 0], wsems, 0, after),
        remote(key_ref, win_ref.at[1, 0], wsems, 1, before),
        remote(val_ref, win_ref.at[0, 1], wsems, 2, after),
        remote(val_ref, win_ref.at[1, 1], wsems, 3, before),
    ]
    for copy in moved:
        copy.start()
    tokens, width = key_ref.shape
    first = lax.axis_index("ctx") * tokens
    line = 0
    for ref in (query_ref, key_ref):
        for start in range(0, tokens, TILE):
            folded = jnp.zeros((TILE, TILE), jnp.float32)
            for column in range(0, width, TILE):
                block = ref[start : start + TILE, column : column + TILE].astype(jnp.float32)
                folded = folded + block * block
            sq_buf[line : line + 1] = jnp.sum(folded.T, axis=0, keepdims=True)
            line += 1
    raw = own_tokens(ids_ref, first, key_ref, val_ref)
    own_squares = jnp.sum(raw * raw, axis=1, keepdims=True)
    sq_buf[4:8] = jnp.broadcast_to(own_squares, (4, TILE))
    squares = sq_buf[...]
    summed = start_all(sq_buf, hslots, hsems, peers)
    total = add_arrivals(squares, hslots, summed)
    total_buf[...] = total
    tot_ref[...] = total
    inverse = lax.rsqrt(total[4:8, 0:1] / D + EPSILON)
    is_key = lax.broadcasted_iota(jnp.int32, raw.shape, 0) < G_DEV
    own_buf[...] = jnp.where(is_key, raw * inverse * gain_ref[1:2], raw).astype(jnp.bfloat16)
    swap = remote(own_buf, glob_ref.at[low, y, z], gsems, 0, other_z)
    swap.start()
    local = pltpu.make_async_copy(own_buf, glob_ref.at[low, y, z], lsem)
    local.start()
    near = [
        remote(total_buf, near_buf.at[0], wsems, 4, after),
        remote(total_buf, near_buf.at[1], wsems, 5, before),
    ]
    for copy in near:
        copy.start()
    local.wait()
    remote(own_buf, glob_ref.at[low, y, 1 - z], gsems, 0, other_z).wait_recv()
    sent = [swap]
    for o, peer in enumerate(y_peers):
        copy = remote(glob_ref.at[low, y], glob_ref.at[low, y], gsems, 1 + o, peer)
        copy.start()
        sent.append(copy)
    for o, peer in enumerate(y_peers):
        source = lax.rem(y + yn - 1 - o, yn)
        remote(glob_ref.at[low, source], glob_ref.at[low, source], gsems, 1 + o, peer).wait_recv()
    for o, peer in enumerate(low_peers):
        copy = remote(glob_ref.at[low], glob_ref.at[low], gsems, yn + o, peer)
        copy.start()
        sent.append(copy)
    for o, peer in enumerate(low_peers):
        source = lax.rem(low + LOW - 1 - o, LOW)
        remote(glob_ref.at[source], glob_ref.at[source], gsems, yn + o, peer).wait_recv()
    for copy in near:
        copy.wait()
    near_ref[...] = near_buf[...]
    for copy in moved:
        copy.wait()
    for copy in sent + summed:
        copy.wait_send()


def spread(ids, query_raw, key_raw, values, gains):
    count = lax.axis_size("ctx")
    heads = lax.axis_size("head")
    yn = count // (LOW * ZN)
    width = key_raw.shape[-1]
    lines = (8, TILE)
    copies = yn + LOW - 1
    vmem = pl.BlockSpec(memory_space=pltpu.VMEM)
    free = pl.BlockSpec(memory_space=pl.ANY)
    return pl.pallas_call(
        functools.partial(spread_kernel, count, heads),
        out_shape=(
            jax.ShapeDtypeStruct((2, 2) + key_raw.shape, jnp.bfloat16),
            jax.ShapeDtypeStruct((LOW, yn, ZN, 2 * G_DEV, width), jnp.bfloat16),
            jax.ShapeDtypeStruct(lines, jnp.float32),
            jax.ShapeDtypeStruct((2,) + lines, jnp.float32),
        ),
        in_specs=[pl.BlockSpec(memory_space=pltpu.SMEM), vmem, vmem, vmem, vmem],
        out_specs=(free, free, vmem, vmem),
        scratch_shapes=[
            pltpu.VMEM(lines, jnp.float32),
            pltpu.VMEM((heads - 1,) + lines, jnp.float32),
            pltpu.VMEM(lines, jnp.float32),
            pltpu.VMEM((2,) + lines, jnp.float32),
            pltpu.VMEM((2 * G_DEV, width), jnp.bfloat16),
            pltpu.SemaphoreType.DMA((6,)),
            pltpu.SemaphoreType.DMA((6,)),
            pltpu.SemaphoreType.DMA((heads - 1,)),
            pltpu.SemaphoreType.DMA((heads - 1,)),
            pltpu.SemaphoreType.DMA((copies,)),
            pltpu.SemaphoreType.DMA((copies,)),
            pltpu.SemaphoreType.DMA,
        ],
        compiler_params=pltpu.CompilerParams(collective_id=1, has_side_effects=True),
    )(ids, query_raw, key_raw, values, gains)


def collect_kernel(
    count, heads, ids_ref, prev_ref, next_ref, part_ref, dots_ref, key_ref, gain_ref,
    from_ref, sum_ref, tot_ref, near_ref, extra_ref,
    slots, half, yslots, quarter, zslot, hslots, total_buf, near_buf, extra_buf, eslots,
    wsend, wrecv, gsend, grecv, hsend, hrecv, esend, erecv,
):
    y, z, low, yn, other_z, y_peers, low_peers, after, before = places(count)
    peers = head_peers(heads)
    greet(peers + [after, before, other_z] + y_peers + low_peers)
    wsems, hsems, gsems, esems = (wsend, wrecv), (hsend, hrecv), (gsend, grecv), (esend, erecv)
    dotted = start_all(dots_ref, hslots, hsems, peers)
    sent = []
    for o, peer in enumerate(low_peers):
        copy = remote(part_ref.at[:, lax.rem(low + 1 + o, LOW)], slots.at[o], gsems, o, peer)
        copy.start()
        sent.append(copy)
    moved = [
        remote(next_ref, from_ref.at[0], wsems, 0, after),
        remote(prev_ref, from_ref.at[1], wsems, 1, before),
    ]
    for copy in moved:
        copy.start()
    total = add_arrivals(dots_ref[...], hslots, dotted)
    total_buf[...] = total
    tot_ref[...] = total
    near = [
        remote(total_buf, near_buf.at[0], wsems, 2, after),
        remote(total_buf, near_buf.at[1], wsems, 3, before),
    ]
    for copy in near:
        copy.start()
    tokens = key_ref.shape[0]
    raw = own_tokens(ids_ref, lax.axis_index("ctx") * tokens, key_ref, key_ref) * gain_ref[1:2]
    summed = add_arrivals(part_ref[:, low], slots, sent)
    each = ZN * G_DEV
    for row in range(yn):
        half[row, 0:each] = summed[0, row * each : (row + 1) * each]
        half[row, each : 2 * each] = summed[1, row * each : (row + 1) * each]
    ysent = []
    for o, peer in enumerate(y_peers):
        copy = remote(half.at[lax.rem(y + 1 + o, yn)], yslots.at[o], gsems, LOW - 1 + o, peer)
        copy.start()
        ysent.append(copy)
    row = add_arrivals(half[y], yslots, ysent)
    quarter[...] = row
    swap = remote(quarter, zslot, gsems, LOW - 1 + yn - 1, other_z)
    swap.start()
    swap.wait_recv()
    reduced = row + zslot[...]
    sum_ref[...] = reduced
    share = jnp.sum(reduced[0:each] * raw, axis=1, keepdims=True)
    extra = jnp.broadcast_to(jnp.concatenate([share, share]), extra_buf.shape)
    extra_buf[...] = extra
    extras = start_all(extra_buf, eslots, esems, peers)
    extra_ref[...] = add_arrivals(extra, eslots, extras)
    for copy in near:
        copy.wait()
    near_ref[...] = near_buf[...]
    for copy in moved:
        copy.wait()
    for copy in sent + ysent + [swap] + dotted + extras:
        copy.wait_send()


def collect(ids, to_prev, to_next, parts, dots, key_raw, gains):
    count = lax.axis_size("ctx")
    heads = lax.axis_size("head")
    yn = count // (LOW * ZN)
    width = parts.shape[-1]
    rows = 2 * ZN * G_DEV
    copies = LOW - 1 + yn
    vmem = pl.BlockSpec(memory_space=pltpu.VMEM)
    free = pl.BlockSpec(memory_space=pl.ANY)
    return pl.pallas_call(
        functools.partial(collect_kernel, count, heads),
        out_shape=(
            jax.ShapeDtypeStruct((2,) + to_prev.shape, jnp.bfloat16),
            jax.ShapeDtypeStruct((rows, width), jnp.float32),
            jax.ShapeDtypeStruct(dots.shape, jnp.float32),
            jax.ShapeDtypeStruct((2,) + dots.shape, jnp.float32),
            jax.ShapeDtypeStruct((rows, 128), jnp.float32),
        ),
        in_specs=[pl.BlockSpec(memory_space=pltpu.SMEM), free, free, vmem, vmem, vmem, vmem],
        out_specs=(free, vmem, vmem, vmem, vmem),
        scratch_shapes=[
            pltpu.VMEM((LOW - 1, 2) + parts.shape[2:], jnp.float32),
            pltpu.VMEM((yn, rows, width), jnp.float32),
            pltpu.VMEM((yn - 1, rows, width), jnp.float32),
            pltpu.VMEM((rows, width), jnp.float32),
            pltpu.VMEM((rows, width), jnp.float32),
            pltpu.VMEM((heads - 1,) + dots.shape, jnp.float32),
            pltpu.VMEM(dots.shape, jnp.float32),
            pltpu.VMEM((2,) + dots.shape, jnp.float32),
            pltpu.VMEM((rows, 128), jnp.float32),
            pltpu.VMEM((heads - 1, rows, 128), jnp.float32),
            pltpu.SemaphoreType.DMA((4,)),
            pltpu.SemaphoreType.DMA((4,)),
            pltpu.SemaphoreType.DMA((copies,)),
            pltpu.SemaphoreType.DMA((copies,)),
            pltpu.SemaphoreType.DMA((heads - 1,)),
            pltpu.SemaphoreType.DMA((heads - 1,)),
            pltpu.SemaphoreType.DMA((heads - 1,)),
            pltpu.SemaphoreType.DMA((heads - 1,)),
        ],
        compiler_params=pltpu.CompilerParams(collective_id=2, has_side_effects=True),
    )(ids, to_prev, to_next, parts, dots, key_raw, gains)


def attention_kernel(
    tiles_ref, readers_ref, tot_ref, near_ref, gain_ref,
    q_ref, g_ref, key_ref, val_ref, win_ref, glob_ref,
    dq_ref, prev_ref, next_ref, own_ref, dglob_ref, dots_ref,
    inverses, queries, keys, vals, dkeys, dvals, dot_sums, live_buf,
):
    tokens = q_ref.shape[0]
    span = KEYS * TILE
    factor = HEAD_DIM ** (-0.5)

    @pl.when(pl.program_id(0) == 0)
    def _():
        own = lax.rsqrt(tot_ref[...] / D + EPSILON)
        near = lax.rsqrt(near_ref[...] / D + EPSILON)
        lines = [own[0:1], own[1:2], near[0, 2:3], near[0, 3:4]]
        lines += [own[2:3], own[3:4], near[1, 2:3], near[1, 3:4]]
        for index, line in enumerate(lines):
            inverses[index * TILE : (index + 1) * TILE] = jnp.broadcast_to(line, (TILE, TILE)).T
        dot_sums[...] = jnp.zeros_like(dot_sums)
        devices = readers_ref.shape[1]
        globals_here = glob_ref.shape[1]
        owner = lax.broadcasted_iota(jnp.int32, (devices, globals_here), 0)
        place = lax.broadcasted_iota(jnp.int32, (devices, globals_here), 1) // G_DEV
        groups = devices // LOW
        match = (owner % LOW == place // groups) & (owner // LOW == place % groups)
        flags = jnp.broadcast_to((readers_ref[...] > 0).astype(jnp.float32), (8, devices))
        live_buf[...] = dot(
            flags.astype(jnp.bfloat16), match.astype(jnp.float32).astype(jnp.bfloat16), ROWS
        )

    qgain = gain_ref[0:1]
    kgain = gain_ref[1:2]
    first_tile = (lax.axis_index("ctx") - 1) * (tokens // TILE)
    last_start = 3 * (tokens // TILE) - KEYS
    query_rows = q_ref[...].astype(jnp.float32)
    queries[...] = (query_rows * inverses[0:tokens] * qgain).astype(jnp.bfloat16)
    blocks = [win_ref[0, 0], key_ref[...], win_ref[1, 0]]
    for index, block in enumerate(blocks):
        rows = slice(index * tokens, (index + 1) * tokens)
        scale = inverses[(index + 1) * tokens : (index + 2) * tokens]
        keys[rows] = (block.astype(jnp.float32) * scale * kgain).astype(jnp.bfloat16)
    vals[0:tokens] = win_ref[0, 1]
    vals[tokens : 2 * tokens] = val_ref[...]
    vals[2 * tokens :] = win_ref[1, 1]
    dkeys[...] = jnp.zeros_like(dkeys)
    dvals[...] = jnp.zeros_like(dvals)
    gkeys = glob_ref[0]
    gvals = glob_ref[1]
    live = live_buf[0:1] > 0
    gdk = 0.0
    gdv = 0.0
    for tile in range(tokens // TILE):
        rows = slice(tile * TILE, (tile + 1) * TILE)
        start = jnp.clip(tiles_ref[tile, 0] - first_tile, 0, last_start)
        window = pl.ds(pl.multiple_of(start * TILE, TILE), span)
        query = queries[rows]
        grad = g_ref[rows]
        wkeys = keys[window]
        wvals = vals[window]
        score_w = dot(query, wkeys, TURNED) * factor
        score_g = jnp.where(live, dot(query, gkeys, TURNED) * factor, -jnp.inf)
        largest = jnp.maximum(
            jnp.max(score_w, axis=1, keepdims=True), jnp.max(score_g, axis=1, keepdims=True)
        )
        exp_w = jnp.exp(score_w - largest)
        exp_g = jnp.exp(score_g - largest)
        inverse = 1.0 / (
            jnp.sum(exp_w, axis=1, keepdims=True) + jnp.sum(exp_g, axis=1, keepdims=True)
        )
        prob_w = exp_w * inverse
        prob_g = exp_g * inverse
        low_w = prob_w.astype(jnp.bfloat16)
        low_g = prob_g.astype(jnp.bfloat16)
        attended = (dot(low_w, wvals, ROWS) + dot(low_g, gvals, ROWS)).astype(jnp.bfloat16)
        delta = jnp.sum(
            grad.astype(jnp.float32) * attended.astype(jnp.float32), axis=1, keepdims=True
        )
        ds_w = (prob_w * (dot(grad, wvals, TURNED) - delta) * factor).astype(jnp.bfloat16)
        ds_g = (prob_g * (dot(grad, gvals, TURNED) - delta) * factor).astype(jnp.bfloat16)
        dq_ref[rows] = dot(ds_w, wkeys, ROWS) + dot(ds_g, gkeys, ROWS)
        dkeys[window] += dot(ds_w, query, DOWN)
        dvals[window] += dot(low_w, grad, DOWN)
        gdk = gdk + dot(ds_g, query, DOWN)
        gdv = gdv + dot(low_g, grad, DOWN)
    for pair_index, cat in enumerate((dkeys, dvals)):
        prev_ref[pair_index] = cat[0:tokens].astype(jnp.bfloat16)
        own_ref[pair_index] = cat[tokens : 2 * tokens]
        next_ref[pair_index] = cat[2 * tokens :].astype(jnp.bfloat16)
    dglob_ref[0] = gdk
    dglob_ref[1] = gdv
    dot_sums[0:tokens] += dq_ref[...] * qgain * query_rows
    for index, block in enumerate(blocks):
        rows = slice(index * tokens, (index + 1) * tokens)
        dot_sums[(index + 1) * tokens : (index + 2) * tokens] += (
            dkeys[rows] * kgain * block.astype(jnp.float32)
        )

    @pl.when(pl.program_id(0) == pl.num_programs(0) - 1)
    def _():
        for index in range(dots_ref.shape[0]):
            turned = dot_sums[index * TILE : (index + 1) * TILE].T
            dots_ref[index : index + 1] = jnp.sum(turned, axis=0, keepdims=True)


def attention(tiles, readers, totals, near, gains, query, out_grad, key, val, window, globs):
    tokens, width = query.shape
    count = globs.shape[1]
    whole = pl.BlockSpec(memory_space=pltpu.VMEM)
    flat = pl.BlockSpec((tokens, HEAD_DIM), lambda h: (0, h))
    gain = pl.BlockSpec((2, HEAD_DIM), lambda h: (0, h))
    pair = pl.BlockSpec((2, tokens, HEAD_DIM), lambda h: (0, 0, h))
    glob = pl.BlockSpec((2, count, HEAD_DIM), lambda h: (0, 0, h))
    pair_shape = (2, tokens, width)
    lines = 4 * tokens // TILE
    return pl.pallas_call(
        attention_kernel,
        grid=(width // HEAD_DIM,),
        out_shape=(
            jax.ShapeDtypeStruct((tokens, width), jnp.float32),
            jax.ShapeDtypeStruct(pair_shape, jnp.bfloat16),
            jax.ShapeDtypeStruct(pair_shape, jnp.bfloat16),
            jax.ShapeDtypeStruct(pair_shape, jnp.float32),
            jax.ShapeDtypeStruct((2, count, width), jnp.float32),
            jax.ShapeDtypeStruct((lines, TILE), jnp.float32),
        ),
        in_specs=[
            pl.BlockSpec(memory_space=pltpu.SMEM),
            whole,
            whole,
            whole,
            gain,
            flat,
            flat,
            flat,
            flat,
            pl.BlockSpec((2, 2, tokens, HEAD_DIM), lambda h: (0, 0, 0, h)),
            glob,
        ],
        out_specs=(flat, pair, pair, pair, glob, pl.BlockSpec((lines, TILE), lambda h: (0, 0))),
        scratch_shapes=[
            pltpu.VMEM((4 * tokens, HEAD_DIM), jnp.float32),
            pltpu.VMEM((tokens, HEAD_DIM), jnp.bfloat16),
            pltpu.VMEM((3 * tokens, HEAD_DIM), jnp.bfloat16),
            pltpu.VMEM((3 * tokens, HEAD_DIM), jnp.bfloat16),
            pltpu.VMEM((3 * tokens, HEAD_DIM), jnp.float32),
            pltpu.VMEM((3 * tokens, HEAD_DIM), jnp.float32),
            pltpu.VMEM((4 * tokens, HEAD_DIM), jnp.float32),
            pltpu.VMEM((8, count), jnp.float32),
        ],
    )(tiles, readers, totals, near, gains, query, out_grad, key, val, window, globs)


def finish_kernel(
    ids_ref, tot_ref, sum_ref, dots_ref, near_ref, extra_ref, gain_ref,
    q_ref, k_ref, dq_ref, own_ref, from_ref, qg_ref, kg_ref, vg_ref, lines,
):
    tokens = q_ref.shape[0]
    device = lax.axis_index("ctx")
    z = lax.rem(device // LOW, ZN)
    spots = lax.broadcasted_iota(jnp.int32, (tokens, HEAD_DIM), 0) + device * tokens

    @pl.when(pl.program_id(0) == 0)
    def _():
        inverse = lax.rsqrt(tot_ref[...] / D + EPSILON)
        dots = dots_ref[...]
        key_dots = dots[4:6] + near_ref[0, 6:8] + near_ref[1, 2:4]
        rows = [inverse[0:1], inverse[1:2], inverse[2:3], inverse[3:4]]
        rows += [dots[0:1], dots[1:2], key_dots[0:1], key_dots[1:2]]
        for index, row in enumerate(rows):
            lines[index * TILE : (index + 1) * TILE] = jnp.broadcast_to(row, (TILE, TILE)).T
        for index in range(G_DEV):
            extra = jnp.where(z == 0, extra_ref[index : index + 1], extra_ref[G_DEV + index : G_DEV + index + 1])
            lines[3 * tokens :] += jnp.where(spots == ids_ref[index], extra, 0.0)

    home_key = own_ref[0] + from_ref[0, 0].astype(jnp.float32) + from_ref[1, 0].astype(jnp.float32)
    home_val = own_ref[1] + from_ref[0, 1].astype(jnp.float32) + from_ref[1, 1].astype(jnp.float32)
    each = ZN * G_DEV
    for index in range(G_DEV):
        here = spots == ids_ref[index]
        other = G_DEV + index
        add_key = jnp.where(z == 0, sum_ref[index : index + 1], sum_ref[other : other + 1])
        add_val = jnp.where(
            z == 0, sum_ref[each + index : each + index + 1], sum_ref[each + other : each + other + 1]
        )
        home_key = home_key + jnp.where(here, add_key, 0.0)
        home_val = home_val + jnp.where(here, add_val, 0.0)
    query_inv = lines[0:tokens]
    key_inv = lines[tokens : 2 * tokens]
    query_dot = lines[2 * tokens : 3 * tokens]
    key_dot = lines[3 * tokens :]
    qg_ref[...] = (
        query_inv * (gain_ref[0:1] * dq_ref[...])
        - q_ref[...].astype(jnp.float32) * (query_inv * query_inv * query_inv) * (query_dot / D)
    ).astype(jnp.bfloat16)
    kg_ref[...] = (
        key_inv * (gain_ref[1:2] * home_key)
        - k_ref[...].astype(jnp.float32) * (key_inv * key_inv * key_inv) * (key_dot / D)
    ).astype(jnp.bfloat16)
    vg_ref[...] = home_val.astype(jnp.bfloat16)


def finish(ids, totals, reduced, dots, near, extra, gains, query, key, dq, own, arrived):
    tokens, width = query.shape
    whole = pl.BlockSpec(memory_space=pltpu.VMEM)
    flat = pl.BlockSpec((tokens, HEAD_DIM), lambda h: (0, h))

    def rows(count):
        return pl.BlockSpec((count, HEAD_DIM), lambda h: (0, h))

    return pl.pallas_call(
        finish_kernel,
        grid=(width // HEAD_DIM,),
        out_shape=(jax.ShapeDtypeStruct((tokens, width), jnp.bfloat16),) * 3,
        in_specs=[
            pl.BlockSpec(memory_space=pltpu.SMEM),
            whole,
            rows(reduced.shape[0]),
            whole,
            whole,
            whole,
            rows(2),
            flat,
            flat,
            flat,
            pl.BlockSpec((2, tokens, HEAD_DIM), lambda h: (0, 0, h)),
            pl.BlockSpec((2, 2, tokens, HEAD_DIM), lambda h: (0, 0, 0, h)),
        ],
        out_specs=(flat,) * 3,
        scratch_shapes=[pltpu.VMEM((4 * tokens, HEAD_DIM), jnp.float32)],
    )(ids, totals, reduced, dots, near, extra, gains, query, key, dq, own, arrived)


def body(
    query_raw, key_raw, values, out_grad, query_gain, key_gain, key_tiles, global_ids, readers
):
    width = query_raw.shape[1]
    count = lax.axis_size("ctx")
    gains = jnp.stack([query_gain, key_gain])
    window, globs, totals, near = spread(global_ids, query_raw, key_raw, values, gains)
    globs = (
        globs.reshape(count, 2, G_DEV, width).transpose(1, 0, 2, 3).reshape(2, count * G_DEV, width)
    )
    grad_query, to_prev, to_next, own_grads, glob_grads, dots = attention(
        key_tiles, readers, totals, near, gains, query_raw, out_grad, key_raw, values, window, globs
    )
    parts = glob_grads.reshape(2, LOW, -1, width)
    arrived, reduced, dot_totals, dot_near, extra = collect(
        global_ids, to_prev, to_next, parts, dots, key_raw, gains
    )
    return tuple(finish(
        global_ids, totals, reduced, dot_totals, dot_near, extra, gains,
        query_raw, key_raw, grad_query, own_grads, arrived,
    ))


def solution(mesh):
    return jax.shard_map(
        body,
        mesh=mesh,
        in_specs=(
            P("ctx", "head"),
            P("ctx", "head"),
            P("ctx", "head"),
            P("ctx", "head"),
            P("head"),
            P("head"),
            P("ctx", None),
            P("ctx"),
            P("ctx", None),
        ),
        out_specs=(P("ctx", "head"), P("ctx", "head"), P("ctx", "head")),
        check_vma=False,
    )
```

```python
import functools

import jax
import jax.numpy as jnp
from jax import lax
from jax.experimental import pallas as pl
from jax.experimental.pallas import tpu as pltpu
from jax.sharding import PartitionSpec as P

HEAD_DIM = 128
D = 5120
TILE = 128
KEYS = 4
G_DEV = 2
MESH = pl.DeviceIdType.MESH

LOW = 8
ZN = 2

EPSILON = 1e-06


def dot(a, b, dims):
    return lax.dot_general(a, b, (dims, ((), ())), preferred_element_type=jnp.float32)


ROWS = ((1,), (0,))
TURNED = ((1,), (1,))
DOWN = ((0,), (0,))


def greet(targets):
    barrier = pltpu.get_barrier_semaphore()
    for target in targets:
        pl.semaphore_signal(barrier, inc=1, device_id=target, device_id_type=MESH)
    pl.semaphore_wait(barrier, len(targets))


def remote(src, dst, sems, index, target):
    return pltpu.make_async_remote_copy(
        src_ref=src,
        dst_ref=dst,
        send_sem=sems[0].at[index],
        recv_sem=sems[1].at[index],
        device_id=target,
        device_id_type=MESH,
    )


def head_peers(heads):
    me = lax.axis_index("head")
    return [{"head": lax.rem(me + o, heads)} for o in range(1, heads)]


def start_all(src, slots, sems, peers):
    copies = [remote(src, slots.at[o], sems, o, peer) for o, peer in enumerate(peers)]
    for copy in copies:
        copy.start()
    return copies


def add_arrivals(total, slots, copies):
    for o, copy in enumerate(copies):
        copy.wait_recv()
        total = total + slots[o]
    return total


def places(count):
    me = lax.axis_index("ctx")
    yn = count // (LOW * ZN)
    low = lax.rem(me, LOW)
    z = lax.rem(me // LOW, ZN)
    y = me // (LOW * ZN)

    def at(y, z, low):
        return {"ctx": (y * ZN + z) * LOW + low}

    other_z = at(y, 1 - z, low)
    y_peers = [at(lax.rem(y + o, yn), z, low) for o in range(1, yn)]
    low_peers = [at(y, z, lax.rem(low + o, LOW)) for o in range(1, LOW)]
    after = {"ctx": lax.rem(me + 1, count)}
    before = {"ctx": lax.rem(me + count - 1, count)}
    return y, z, low, yn, other_z, y_peers, low_peers, after, before


def own_tokens(ids_ref, first, key_ref, val_ref):
    tokens = key_ref.shape[0]
    rows = lax.broadcasted_iota(jnp.int32, (8, tokens), 0)
    spots = lax.broadcasted_iota(jnp.int32, (8, tokens), 1)
    picks = jnp.zeros((8, tokens), jnp.float32)
    for index in range(G_DEV):
        hit = (rows % G_DEV == index) & (spots == ids_ref[index] - first)
        picks = jnp.where(hit, 1.0, picks)
    picks = picks.astype(jnp.bfloat16)
    keys = dot(picks, key_ref[...], ROWS)[0:4]
    vals = dot(picks, val_ref[...], ROWS)[0:4]
    is_key = lax.broadcasted_iota(jnp.int32, keys.shape, 0) < G_DEV
    return jnp.where(is_key, keys, vals)


def spread_kernel(
    count, heads, ids_ref, query_ref, key_ref, val_ref, qgain_ref, kgain_ref,
    win_ref, glob_ref, tot_ref, near_ref, gain_ref,
    sq_buf, hslots, total_buf, near_buf, own_buf, wsend, wrecv, hsend, hrecv, gsend, grecv, lsem,
):
    y, z, low, yn, other_z, y_peers, low_peers, after, before = places(count)
    peers = head_peers(heads)
    greet(peers + [after, before, other_z] + y_peers + low_peers)
    wsems, hsems, gsems = (wsend, wrecv), (hsend, hrecv), (gsend, grecv)
    tokens, width = key_ref.shape
    early = pl.ds(0, TILE)
    rest = pl.ds(TILE, tokens - TILE)
    moved = [
        remote(key_ref.at[early], win_ref.at[0, 0, early], wsems, 0, after),
        remote(key_ref.at[early], win_ref.at[1, 0, early], wsems, 1, before),
        remote(key_ref.at[rest], win_ref.at[0, 0, rest], wsems, 2, after),
        remote(key_ref.at[rest], win_ref.at[1, 0, rest], wsems, 3, before),
        remote(val_ref, win_ref.at[0, 1], wsems, 4, after),
        remote(val_ref, win_ref.at[1, 1], wsems, 5, before),
    ]
    for copy in moved[:2]:
        copy.start()
    first = lax.axis_index("ctx") * tokens
    line = 0
    for ref in (query_ref, key_ref):
        for start in range(0, tokens, TILE):
            folded = jnp.zeros((TILE, TILE), jnp.float32)
            for column in range(0, width, TILE):
                block = ref[start : start + TILE, column : column + TILE].astype(jnp.float32)
                folded = folded + block * block
            sq_buf[line : line + 1] = jnp.sum(folded.T, axis=0, keepdims=True)
            line += 1
    kgain = kgain_ref[...].reshape(1, width)
    gain_ref[0:1] = qgain_ref[...].reshape(1, width)
    gain_ref[1:2] = kgain
    raw = own_tokens(ids_ref, first, key_ref, val_ref)
    own_squares = jnp.sum(raw * raw, axis=1, keepdims=True)
    sq_buf[4:8] = jnp.broadcast_to(own_squares, (4, TILE))
    squares = sq_buf[...]
    summed = start_all(sq_buf, hslots, hsems, peers)
    total = add_arrivals(squares, hslots, summed)
    total_buf[...] = total
    tot_ref[...] = total
    inverse = lax.rsqrt(total[4:8, 0:1] / D + EPSILON)
    is_key = lax.broadcasted_iota(jnp.int32, raw.shape, 0) < G_DEV
    own_buf[...] = jnp.where(is_key, raw * inverse * kgain, raw).astype(jnp.bfloat16)
    swap = remote(own_buf, glob_ref.at[low, y, z], gsems, 0, other_z)
    swap.start()
    local = pltpu.make_async_copy(own_buf, glob_ref.at[low, y, z], lsem)
    local.start()
    near = [
        remote(total_buf, near_buf.at[0], wsems, 6, after),
        remote(total_buf, near_buf.at[1], wsems, 7, before),
    ]
    for copy in near + moved[2:]:
        copy.start()
    local.wait()
    remote(own_buf, glob_ref.at[low, y, 1 - z], gsems, 0, other_z).wait_recv()
    sent = [swap]
    for o, peer in enumerate(y_peers):
        copy = remote(glob_ref.at[low, y], glob_ref.at[low, y], gsems, 1 + o, peer)
        copy.start()
        sent.append(copy)
    for o, peer in enumerate(y_peers):
        source = lax.rem(y + yn - 1 - o, yn)
        remote(glob_ref.at[low, source], glob_ref.at[low, source], gsems, 1 + o, peer).wait_recv()
    for o, peer in enumerate(low_peers):
        copy = remote(glob_ref.at[low], glob_ref.at[low], gsems, yn + o, peer)
        copy.start()
        sent.append(copy)
    for o, peer in enumerate(low_peers):
        source = lax.rem(low + LOW - 1 - o, LOW)
        remote(glob_ref.at[source], glob_ref.at[source], gsems, yn + o, peer).wait_recv()
    for copy in near:
        copy.wait()
    near_ref[...] = near_buf[...]
    for copy in moved:
        copy.wait()
    for copy in sent + summed:
        copy.wait_send()


def spread(ids, query_raw, key_raw, values, query_gain, key_gain):
    count = lax.axis_size("ctx")
    heads = lax.axis_size("head")
    yn = count // (LOW * ZN)
    width = key_raw.shape[-1]
    lines = (8, TILE)
    copies = yn + LOW - 1
    vmem = pl.BlockSpec(memory_space=pltpu.VMEM)
    free = pl.BlockSpec(memory_space=pl.ANY)
    return pl.pallas_call(
        functools.partial(spread_kernel, count, heads),
        out_shape=(
            jax.ShapeDtypeStruct((2, 2) + key_raw.shape, jnp.bfloat16),
            jax.ShapeDtypeStruct((LOW, yn, ZN, 2 * G_DEV, width), jnp.bfloat16),
            jax.ShapeDtypeStruct(lines, jnp.float32),
            jax.ShapeDtypeStruct((2,) + lines, jnp.float32),
            jax.ShapeDtypeStruct((2, width), jnp.float32),
        ),
        in_specs=[pl.BlockSpec(memory_space=pltpu.SMEM), vmem, vmem, vmem, vmem, vmem],
        out_specs=(free, free, vmem, vmem, vmem),
        scratch_shapes=[
            pltpu.VMEM(lines, jnp.float32),
            pltpu.VMEM((heads - 1,) + lines, jnp.float32),
            pltpu.VMEM(lines, jnp.float32),
            pltpu.VMEM((2,) + lines, jnp.float32),
            pltpu.VMEM((2 * G_DEV, width), jnp.bfloat16),
            pltpu.SemaphoreType.DMA((8,)),
            pltpu.SemaphoreType.DMA((8,)),
            pltpu.SemaphoreType.DMA((heads - 1,)),
            pltpu.SemaphoreType.DMA((heads - 1,)),
            pltpu.SemaphoreType.DMA((copies,)),
            pltpu.SemaphoreType.DMA((copies,)),
            pltpu.SemaphoreType.DMA,
        ],
        compiler_params=pltpu.CompilerParams(collective_id=1, has_side_effects=True),
    )(ids, query_raw, key_raw, values, query_gain, key_gain)


def collect_kernel(
    count, heads, ids_ref, prev_ref, next_ref, part_ref, dots_ref, key_ref, gain_ref,
    from_ref, sum_ref, tot_ref, near_ref, extra_ref,
    slots, half, yslots, quarter, zslot, hslots, total_buf, near_buf, extra_buf, eslots,
    wsend, wrecv, gsend, grecv, hsend, hrecv, esend, erecv,
):
    y, z, low, yn, other_z, y_peers, low_peers, after, before = places(count)
    peers = head_peers(heads)
    greet(peers + [after, before, other_z] + y_peers + low_peers)
    wsems, hsems, gsems, esems = (wsend, wrecv), (hsend, hrecv), (gsend, grecv), (esend, erecv)
    dotted = start_all(dots_ref, hslots, hsems, peers)
    sent = []
    for o, peer in enumerate(low_peers):
        copy = remote(part_ref.at[:, lax.rem(low + 1 + o, LOW)], slots.at[o], gsems, o, peer)
        copy.start()
        sent.append(copy)
    tokens = key_ref.shape[0]
    upper = pl.ds(0, TILE)
    lower = pl.ds(TILE, tokens - TILE)
    moved = [
        remote(next_ref.at[0], from_ref.at[0, 0], wsems, 0, after),
        remote(prev_ref.at[0], from_ref.at[1, 0], wsems, 1, before),
        remote(next_ref.at[1, upper], from_ref.at[0, 1, upper], wsems, 4, after),
        remote(prev_ref.at[1, upper], from_ref.at[1, 1, upper], wsems, 5, before),
        remote(next_ref.at[1, lower], from_ref.at[0, 1, lower], wsems, 6, after),
        remote(prev_ref.at[1, lower], from_ref.at[1, 1, lower], wsems, 7, before),
    ]
    for copy in moved[:2]:
        copy.start()
    total = add_arrivals(dots_ref[...], hslots, dotted)
    total_buf[...] = total
    tot_ref[...] = total
    near = [
        remote(total_buf, near_buf.at[0], wsems, 2, after),
        remote(total_buf, near_buf.at[1], wsems, 3, before),
    ]
    for copy in near:
        copy.start()
    raw = own_tokens(ids_ref, lax.axis_index("ctx") * tokens, key_ref, key_ref) * gain_ref[1:2]
    summed = add_arrivals(part_ref[:, low], slots, sent)
    each = ZN * G_DEV
    for row in range(yn):
        half[row, 0:each] = summed[0, row * each : (row + 1) * each]
        half[row, each : 2 * each] = summed[1, row * each : (row + 1) * each]
    ysent = []
    for o, peer in enumerate(y_peers):
        copy = remote(half.at[lax.rem(y + 1 + o, yn)], yslots.at[o], gsems, LOW - 1 + o, peer)
        copy.start()
        ysent.append(copy)
    row = add_arrivals(half[y], yslots, ysent)
    quarter[...] = row
    swap = remote(quarter, zslot, gsems, LOW - 1 + yn - 1, other_z)
    for copy in [swap] + moved[2:4]:
        copy.start()
    swap.wait_recv()
    reduced = row + zslot[...]
    sum_ref[...] = reduced
    share = jnp.sum(reduced[0:each] * raw, axis=1, keepdims=True)
    extra = jnp.broadcast_to(jnp.concatenate([share, share]), extra_buf.shape)
    extra_buf[...] = extra
    extras = start_all(extra_buf, eslots, esems, peers)
    for copy in moved[4:]:
        copy.start()
    extra_ref[...] = add_arrivals(extra, eslots, extras)
    for copy in near:
        copy.wait()
    near_ref[...] = near_buf[...]
    for copy in moved:
        copy.wait()
    for copy in sent + ysent + [swap] + dotted + extras:
        copy.wait_send()


def collect(ids, to_prev, to_next, parts, dots, key_raw, gains):
    count = lax.axis_size("ctx")
    heads = lax.axis_size("head")
    yn = count // (LOW * ZN)
    width = parts.shape[-1]
    rows = 2 * ZN * G_DEV
    copies = LOW - 1 + yn
    vmem = pl.BlockSpec(memory_space=pltpu.VMEM)
    free = pl.BlockSpec(memory_space=pl.ANY)
    return pl.pallas_call(
        functools.partial(collect_kernel, count, heads),
        out_shape=(
            jax.ShapeDtypeStruct((2,) + to_prev.shape, jnp.bfloat16),
            jax.ShapeDtypeStruct((rows, width), jnp.float32),
            jax.ShapeDtypeStruct(dots.shape, jnp.float32),
            jax.ShapeDtypeStruct((2,) + dots.shape, jnp.float32),
            jax.ShapeDtypeStruct((rows, 128), jnp.float32),
        ),
        in_specs=[pl.BlockSpec(memory_space=pltpu.SMEM), free, free, vmem, vmem, vmem, vmem],
        out_specs=(free, vmem, vmem, vmem, vmem),
        scratch_shapes=[
            pltpu.VMEM((LOW - 1, 2) + parts.shape[2:], jnp.float32),
            pltpu.VMEM((yn, rows, width), jnp.float32),
            pltpu.VMEM((yn - 1, rows, width), jnp.float32),
            pltpu.VMEM((rows, width), jnp.float32),
            pltpu.VMEM((rows, width), jnp.float32),
            pltpu.VMEM((heads - 1,) + dots.shape, jnp.float32),
            pltpu.VMEM(dots.shape, jnp.float32),
            pltpu.VMEM((2,) + dots.shape, jnp.float32),
            pltpu.VMEM((rows, 128), jnp.float32),
            pltpu.VMEM((heads - 1, rows, 128), jnp.float32),
            pltpu.SemaphoreType.DMA((8,)),
            pltpu.SemaphoreType.DMA((8,)),
            pltpu.SemaphoreType.DMA((copies,)),
            pltpu.SemaphoreType.DMA((copies,)),
            pltpu.SemaphoreType.DMA((heads - 1,)),
            pltpu.SemaphoreType.DMA((heads - 1,)),
            pltpu.SemaphoreType.DMA((heads - 1,)),
            pltpu.SemaphoreType.DMA((heads - 1,)),
        ],
        compiler_params=pltpu.CompilerParams(collective_id=2, has_side_effects=True),
    )(ids, to_prev, to_next, parts, dots, key_raw, gains)


def attention_kernel(
    tiles_ref, readers_ref, tot_ref, near_ref, gain_ref,
    q_ref, g_ref, key_ref, val_ref, win_ref, glob_ref,
    dq_ref, prev_ref, next_ref, own_ref, dglob_ref, dots_ref,
    inverses, queries, keys, vals, dkeys, dvals, dot_sums, live_buf,
):
    tokens = q_ref.shape[0]
    span = KEYS * TILE
    factor = HEAD_DIM ** (-0.5)

    @pl.when(pl.program_id(0) == 0)
    def _():
        own = lax.rsqrt(tot_ref[...] / D + EPSILON)
        near = lax.rsqrt(near_ref[...] / D + EPSILON)
        lines = [own[0:1], own[1:2], near[0, 2:3], near[0, 3:4]]
        lines += [own[2:3], own[3:4], near[1, 2:3], near[1, 3:4]]
        for index, line in enumerate(lines):
            inverses[index * TILE : (index + 1) * TILE] = jnp.broadcast_to(line, (TILE, TILE)).T
        dot_sums[...] = jnp.zeros_like(dot_sums)
        devices = readers_ref.shape[1]
        globals_here = glob_ref.shape[1]
        owner = lax.broadcasted_iota(jnp.int32, (devices, globals_here), 0)
        place = lax.broadcasted_iota(jnp.int32, (devices, globals_here), 1) // G_DEV
        groups = devices // LOW
        match = (owner % LOW == place // groups) & (owner // LOW == place % groups)
        flags = jnp.broadcast_to((readers_ref[...] > 0).astype(jnp.float32), (8, devices))
        live_buf[...] = dot(
            flags.astype(jnp.bfloat16), match.astype(jnp.float32).astype(jnp.bfloat16), ROWS
        )

    qgain = gain_ref[0:1]
    kgain = gain_ref[1:2]
    first_tile = (lax.axis_index("ctx") - 1) * (tokens // TILE)
    last_start = 3 * (tokens // TILE) - KEYS
    query_rows = q_ref[...].astype(jnp.float32)
    queries[...] = (query_rows * inverses[0:tokens] * qgain).astype(jnp.bfloat16)
    blocks = [win_ref[0, 0], key_ref[...], win_ref[1, 0]]
    for index, block in enumerate(blocks):
        rows = slice(index * tokens, (index + 1) * tokens)
        scale = inverses[(index + 1) * tokens : (index + 2) * tokens]
        keys[rows] = (block.astype(jnp.float32) * scale * kgain).astype(jnp.bfloat16)
    vals[0:tokens] = win_ref[0, 1]
    vals[tokens : 2 * tokens] = val_ref[...]
    vals[2 * tokens :] = win_ref[1, 1]
    dkeys[...] = jnp.zeros_like(dkeys)
    dvals[...] = jnp.zeros_like(dvals)
    gkeys = glob_ref[0]
    gvals = glob_ref[1]
    live = live_buf[0:1] > 0
    gdk = 0.0
    gdv = 0.0
    for tile in range(tokens // TILE):
        rows = slice(tile * TILE, (tile + 1) * TILE)
        start = jnp.clip(tiles_ref[tile, 0] - first_tile, 0, last_start)
        window = pl.ds(pl.multiple_of(start * TILE, TILE), span)
        query = queries[rows]
        grad = g_ref[rows]
        wkeys = keys[window]
        wvals = vals[window]
        score_w = dot(query, wkeys, TURNED) * factor
        score_g = jnp.where(live, dot(query, gkeys, TURNED) * factor, -jnp.inf)
        largest = jnp.maximum(
            jnp.max(score_w, axis=1, keepdims=True), jnp.max(score_g, axis=1, keepdims=True)
        )
        exp_w = jnp.exp(score_w - largest)
        exp_g = jnp.exp(score_g - largest)
        inverse = 1.0 / (
            jnp.sum(exp_w, axis=1, keepdims=True) + jnp.sum(exp_g, axis=1, keepdims=True)
        )
        prob_w = exp_w * inverse
        prob_g = exp_g * inverse
        low_w = prob_w.astype(jnp.bfloat16)
        low_g = prob_g.astype(jnp.bfloat16)
        attended = (dot(low_w, wvals, ROWS) + dot(low_g, gvals, ROWS)).astype(jnp.bfloat16)
        delta = jnp.sum(
            grad.astype(jnp.float32) * attended.astype(jnp.float32), axis=1, keepdims=True
        )
        ds_w = (prob_w * (dot(grad, wvals, TURNED) - delta) * factor).astype(jnp.bfloat16)
        ds_g = (prob_g * (dot(grad, gvals, TURNED) - delta) * factor).astype(jnp.bfloat16)
        dq_ref[rows] = dot(ds_w, wkeys, ROWS) + dot(ds_g, gkeys, ROWS)
        dkeys[window] += dot(ds_w, query, DOWN)
        dvals[window] += dot(low_w, grad, DOWN)
        gdk = gdk + dot(ds_g, query, DOWN)
        gdv = gdv + dot(low_g, grad, DOWN)
    for pair_index, cat in enumerate((dkeys, dvals)):
        prev_ref[pair_index] = cat[0:tokens].astype(jnp.bfloat16)
        own_ref[pair_index] = cat[tokens : 2 * tokens]
        next_ref[pair_index] = cat[2 * tokens :].astype(jnp.bfloat16)
    dglob_ref[0] = gdk
    dglob_ref[1] = gdv
    dot_sums[0:tokens] += dq_ref[...] * qgain * query_rows
    for index, block in enumerate(blocks):
        rows = slice(index * tokens, (index + 1) * tokens)
        dot_sums[(index + 1) * tokens : (index + 2) * tokens] += (
            dkeys[rows] * kgain * block.astype(jnp.float32)
        )

    @pl.when(pl.program_id(0) == pl.num_programs(0) - 1)
    def _():
        for index in range(dots_ref.shape[0]):
            turned = dot_sums[index * TILE : (index + 1) * TILE].T
            dots_ref[index : index + 1] = jnp.sum(turned, axis=0, keepdims=True)


def attention(tiles, readers, totals, near, gains, query, out_grad, key, val, window, globs):
    tokens, width = query.shape
    count = globs.shape[1]
    whole = pl.BlockSpec(memory_space=pltpu.VMEM)
    flat = pl.BlockSpec((tokens, HEAD_DIM), lambda h: (0, h))
    gain = pl.BlockSpec((2, HEAD_DIM), lambda h: (0, h))
    pair = pl.BlockSpec((2, tokens, HEAD_DIM), lambda h: (0, 0, h))
    glob = pl.BlockSpec((2, count, HEAD_DIM), lambda h: (0, 0, h))
    pair_shape = (2, tokens, width)
    lines = 4 * tokens // TILE
    return pl.pallas_call(
        attention_kernel,
        grid=(width // HEAD_DIM,),
        out_shape=(
            jax.ShapeDtypeStruct((tokens, width), jnp.float32),
            jax.ShapeDtypeStruct(pair_shape, jnp.bfloat16),
            jax.ShapeDtypeStruct(pair_shape, jnp.bfloat16),
            jax.ShapeDtypeStruct(pair_shape, jnp.float32),
            jax.ShapeDtypeStruct((2, count, width), jnp.float32),
            jax.ShapeDtypeStruct((lines, TILE), jnp.float32),
        ),
        in_specs=[
            pl.BlockSpec(memory_space=pltpu.SMEM),
            whole,
            whole,
            whole,
            gain,
            flat,
            flat,
            flat,
            flat,
            pl.BlockSpec((2, 2, tokens, HEAD_DIM), lambda h: (0, 0, 0, h)),
            glob,
        ],
        out_specs=(flat, pair, pair, pair, glob, pl.BlockSpec((lines, TILE), lambda h: (0, 0))),
        scratch_shapes=[
            pltpu.VMEM((4 * tokens, HEAD_DIM), jnp.float32),
            pltpu.VMEM((tokens, HEAD_DIM), jnp.bfloat16),
            pltpu.VMEM((3 * tokens, HEAD_DIM), jnp.bfloat16),
            pltpu.VMEM((3 * tokens, HEAD_DIM), jnp.bfloat16),
            pltpu.VMEM((3 * tokens, HEAD_DIM), jnp.float32),
            pltpu.VMEM((3 * tokens, HEAD_DIM), jnp.float32),
            pltpu.VMEM((4 * tokens, HEAD_DIM), jnp.float32),
            pltpu.VMEM((8, count), jnp.float32),
        ],
    )(tiles, readers, totals, near, gains, query, out_grad, key, val, window, globs)


def finish_kernel(
    ids_ref, tot_ref, sum_ref, dots_ref, near_ref, extra_ref, gain_ref,
    q_ref, k_ref, dq_ref, own_ref, from_ref, qg_ref, kg_ref, vg_ref, lines,
):
    tokens = q_ref.shape[0]
    device = lax.axis_index("ctx")
    z = lax.rem(device // LOW, ZN)
    spots = lax.broadcasted_iota(jnp.int32, (tokens, HEAD_DIM), 0) + device * tokens

    @pl.when(pl.program_id(0) == 0)
    def _():
        inverse = lax.rsqrt(tot_ref[...] / D + EPSILON)
        dots = dots_ref[...]
        key_dots = dots[4:6] + near_ref[0, 6:8] + near_ref[1, 2:4]
        rows = [inverse[0:1], inverse[1:2], inverse[2:3], inverse[3:4]]
        rows += [dots[0:1], dots[1:2], key_dots[0:1], key_dots[1:2]]
        for index, row in enumerate(rows):
            lines[index * TILE : (index + 1) * TILE] = jnp.broadcast_to(row, (TILE, TILE)).T
        for index in range(G_DEV):
            extra = jnp.where(z == 0, extra_ref[index : index + 1], extra_ref[G_DEV + index : G_DEV + index + 1])
            lines[3 * tokens :] += jnp.where(spots == ids_ref[index], extra, 0.0)

    home_key = own_ref[0] + from_ref[0, 0].astype(jnp.float32) + from_ref[1, 0].astype(jnp.float32)
    home_val = own_ref[1] + from_ref[0, 1].astype(jnp.float32) + from_ref[1, 1].astype(jnp.float32)
    each = ZN * G_DEV
    for index in range(G_DEV):
        here = spots == ids_ref[index]
        other = G_DEV + index
        add_key = jnp.where(z == 0, sum_ref[index : index + 1], sum_ref[other : other + 1])
        add_val = jnp.where(
            z == 0, sum_ref[each + index : each + index + 1], sum_ref[each + other : each + other + 1]
        )
        home_key = home_key + jnp.where(here, add_key, 0.0)
        home_val = home_val + jnp.where(here, add_val, 0.0)
    query_inv = lines[0:tokens]
    key_inv = lines[tokens : 2 * tokens]
    query_dot = lines[2 * tokens : 3 * tokens]
    key_dot = lines[3 * tokens :]
    qg_ref[...] = (
        query_inv * (gain_ref[0:1] * dq_ref[...])
        - q_ref[...].astype(jnp.float32) * (query_inv * query_inv * query_inv) * (query_dot / D)
    ).astype(jnp.bfloat16)
    kg_ref[...] = (
        key_inv * (gain_ref[1:2] * home_key)
        - k_ref[...].astype(jnp.float32) * (key_inv * key_inv * key_inv) * (key_dot / D)
    ).astype(jnp.bfloat16)
    vg_ref[...] = home_val.astype(jnp.bfloat16)


def finish(ids, totals, reduced, dots, near, extra, gains, query, key, dq, own, arrived):
    tokens, width = query.shape
    whole = pl.BlockSpec(memory_space=pltpu.VMEM)
    flat = pl.BlockSpec((tokens, HEAD_DIM), lambda h: (0, h))

    def rows(count):
        return pl.BlockSpec((count, HEAD_DIM), lambda h: (0, h))

    return pl.pallas_call(
        finish_kernel,
        grid=(width // HEAD_DIM,),
        out_shape=(jax.ShapeDtypeStruct((tokens, width), jnp.bfloat16),) * 3,
        in_specs=[
            pl.BlockSpec(memory_space=pltpu.SMEM),
            whole,
            rows(reduced.shape[0]),
            whole,
            whole,
            whole,
            rows(2),
            flat,
            flat,
            flat,
            pl.BlockSpec((2, tokens, HEAD_DIM), lambda h: (0, 0, h)),
            pl.BlockSpec((2, 2, tokens, HEAD_DIM), lambda h: (0, 0, 0, h)),
        ],
        out_specs=(flat,) * 3,
        scratch_shapes=[pltpu.VMEM((4 * tokens, HEAD_DIM), jnp.float32)],
    )(ids, totals, reduced, dots, near, extra, gains, query, key, dq, own, arrived)


def body(
    query_raw, key_raw, values, out_grad, query_gain, key_gain, key_tiles, global_ids, readers
):
    width = query_raw.shape[1]
    count = lax.axis_size("ctx")
    window, globs, totals, near, gains = spread(
        global_ids, query_raw, key_raw, values, query_gain, key_gain
    )
    globs = (
        globs.reshape(count, 2, G_DEV, width).transpose(1, 0, 2, 3).reshape(2, count * G_DEV, width)
    )
    grad_query, to_prev, to_next, own_grads, glob_grads, dots = attention(
        key_tiles, readers, totals, near, gains, query_raw, out_grad, key_raw, values, window, globs
    )
    parts = glob_grads.reshape(2, LOW, -1, width)
    arrived, reduced, dot_totals, dot_near, extra = collect(
        global_ids, to_prev, to_next, parts, dots, key_raw, gains
    )
    return tuple(finish(
        global_ids, totals, reduced, dot_totals, dot_near, extra, gains,
        query_raw, key_raw, grad_query, own_grads, arrived,
    ))


def solution(mesh):
    return jax.shard_map(
        body,
        mesh=mesh,
        in_specs=(
            P("ctx", "head"),
            P("ctx", "head"),
            P("ctx", "head"),
            P("ctx", "head"),
            P("head"),
            P("head"),
            P("ctx", None),
            P("ctx"),
            P("ctx", None),
        ),
        out_specs=(P("ctx", "head"), P("ctx", "head"), P("ctx", "head")),
        check_vma=False,
    )
```

```python
import functools

import jax
import jax.numpy as jnp
from jax import lax
from jax.experimental import pallas as pl
from jax.experimental.pallas import tpu as pltpu
from jax.sharding import PartitionSpec as P

HEAD_DIM = 128
D = 5120
TILE = 128
KEYS = 4
G_DEV = 2
MESH = pl.DeviceIdType.MESH

LOW = 8
ZN = 2

EPSILON = 1e-06


def dot(a, b, dims):
    return lax.dot_general(a, b, (dims, ((), ())), preferred_element_type=jnp.float32)


ROWS = ((1,), (0,))
TURNED = ((1,), (1,))
DOWN = ((0,), (0,))


def greet(targets):
    barrier = pltpu.get_barrier_semaphore()
    for target in targets:
        pl.semaphore_signal(barrier, inc=1, device_id=target, device_id_type=MESH)
    pl.semaphore_wait(barrier, len(targets))


def remote(src, dst, sems, index, target):
    return pltpu.make_async_remote_copy(
        src_ref=src,
        dst_ref=dst,
        send_sem=sems[0].at[index],
        recv_sem=sems[1].at[index],
        device_id=target,
        device_id_type=MESH,
    )


def head_peers(heads):
    me = lax.axis_index("head")
    return [{"head": lax.rem(me + o, heads)} for o in range(1, heads)]


def start_all(src, slots, sems, peers):
    copies = [remote(src, slots.at[o], sems, o, peer) for o, peer in enumerate(peers)]
    for copy in copies:
        copy.start()
    return copies


def add_arrivals(total, slots, copies):
    for o, copy in enumerate(copies):
        copy.wait_recv()
        total = total + slots[o]
    return total


def places(count):
    me = lax.axis_index("ctx")
    yn = count // (LOW * ZN)
    low = lax.rem(me, LOW)
    z = lax.rem(me // LOW, ZN)
    y = me // (LOW * ZN)

    def at(y, z, low):
        return {"ctx": (y * ZN + z) * LOW + low}

    other_z = at(y, 1 - z, low)
    y_peers = [at(lax.rem(y + o, yn), z, low) for o in range(1, yn)]
    low_peers = [at(y, z, lax.rem(low + o, LOW)) for o in range(1, LOW)]
    after = {"ctx": lax.rem(me + 1, count)}
    before = {"ctx": lax.rem(me + count - 1, count)}
    return y, z, low, yn, other_z, y_peers, low_peers, after, before


def own_tokens(ids_ref, first, key_ref, val_ref):
    tokens = key_ref.shape[0]
    rows = lax.broadcasted_iota(jnp.int32, (8, tokens), 0)
    spots = lax.broadcasted_iota(jnp.int32, (8, tokens), 1)
    picks = jnp.zeros((8, tokens), jnp.float32)
    for index in range(G_DEV):
        hit = (rows % G_DEV == index) & (spots == ids_ref[index] - first)
        picks = jnp.where(hit, 1.0, picks)
    picks = picks.astype(jnp.bfloat16)
    keys = dot(picks, key_ref[...], ROWS)[0:4]
    vals = dot(picks, val_ref[...], ROWS)[0:4]
    is_key = lax.broadcasted_iota(jnp.int32, keys.shape, 0) < G_DEV
    return jnp.where(is_key, keys, vals)


def spread_kernel(
    count, heads, ids_ref, query_ref, key_ref, val_ref, qgain_ref, kgain_ref,
    win_ref, glob_ref, tot_ref, near_ref, gain_ref,
    sq_buf, hslots, total_buf, near_buf, own_buf, wsend, wrecv, hsend, hrecv, gsend, grecv, lsem,
):
    y, z, low, yn, other_z, y_peers, low_peers, after, before = places(count)
    peers = head_peers(heads)
    greet(peers + [after, before, other_z] + y_peers + low_peers)
    wsems, hsems, gsems = (wsend, wrecv), (hsend, hrecv), (gsend, grecv)
    tokens, width = key_ref.shape
    early = pl.ds(0, TILE // 2)
    rest = pl.ds(TILE // 2, tokens - TILE // 2)
    moved = [
        remote(key_ref.at[early], win_ref.at[0, 0, early], wsems, 0, after),
        remote(key_ref.at[early], win_ref.at[1, 0, early], wsems, 1, before),
        remote(key_ref.at[rest], win_ref.at[0, 0, rest], wsems, 2, after),
        remote(key_ref.at[rest], win_ref.at[1, 0, rest], wsems, 3, before),
        remote(val_ref, win_ref.at[0, 1], wsems, 4, after),
        remote(val_ref, win_ref.at[1, 1], wsems, 5, before),
    ]
    for copy in moved[:2]:
        copy.start()
    first = lax.axis_index("ctx") * tokens
    line = 0
    for ref in (query_ref, key_ref):
        for start in range(0, tokens, TILE):
            folded = jnp.zeros((TILE, TILE), jnp.float32)
            for column in range(0, width, TILE):
                block = ref[start : start + TILE, column : column + TILE].astype(jnp.float32)
                folded = folded + block * block
            sq_buf[line : line + 1] = jnp.sum(folded.T, axis=0, keepdims=True)
            line += 1
    kgain = kgain_ref[...].reshape(1, width)
    gain_ref[0:1] = qgain_ref[...].reshape(1, width)
    gain_ref[1:2] = kgain
    raw = own_tokens(ids_ref, first, key_ref, val_ref)
    own_squares = jnp.sum(raw * raw, axis=1, keepdims=True)
    sq_buf[4:8] = jnp.broadcast_to(own_squares, (4, TILE))
    squares = sq_buf[...]
    summed = start_all(sq_buf, hslots, hsems, peers)
    total = add_arrivals(squares, hslots, summed)
    total_buf[...] = total
    tot_ref[...] = total
    inverse = lax.rsqrt(total[4:8, 0:1] / D + EPSILON)
    is_key = lax.broadcasted_iota(jnp.int32, raw.shape, 0) < G_DEV
    own_buf[...] = jnp.where(is_key, raw * inverse * kgain, raw).astype(jnp.bfloat16)
    swap = remote(own_buf, glob_ref.at[low, y, z], gsems, 0, other_z)
    swap.start()
    local = pltpu.make_async_copy(own_buf, glob_ref.at[low, y, z], lsem)
    local.start()
    near = [
        remote(total_buf, near_buf.at[0], wsems, 6, after),
        remote(total_buf, near_buf.at[1], wsems, 7, before),
    ]
    for copy in near + moved[2:]:
        copy.start()
    local.wait()
    remote(own_buf, glob_ref.at[low, y, 1 - z], gsems, 0, other_z).wait_recv()
    sent = [swap]
    for o, peer in enumerate(y_peers):
        copy = remote(glob_ref.at[low, y], glob_ref.at[low, y], gsems, 1 + o, peer)
        copy.start()
        sent.append(copy)
    for o, peer in enumerate(y_peers):
        source = lax.rem(y + yn - 1 - o, yn)
        remote(glob_ref.at[low, source], glob_ref.at[low, source], gsems, 1 + o, peer).wait_recv()
    for o, peer in enumerate(low_peers):
        copy = remote(glob_ref.at[low], glob_ref.at[low], gsems, yn + o, peer)
        copy.start()
        sent.append(copy)
    for o, peer in enumerate(low_peers):
        source = lax.rem(low + LOW - 1 - o, LOW)
        remote(glob_ref.at[source], glob_ref.at[source], gsems, yn + o, peer).wait_recv()
    for copy in near:
        copy.wait()
    near_ref[...] = near_buf[...]
    for copy in moved:
        copy.wait()
    for copy in sent + summed:
        copy.wait_send()


def spread(ids, query_raw, key_raw, values, query_gain, key_gain):
    count = lax.axis_size("ctx")
    heads = lax.axis_size("head")
    yn = count // (LOW * ZN)
    width = key_raw.shape[-1]
    lines = (8, TILE)
    copies = yn + LOW - 1
    vmem = pl.BlockSpec(memory_space=pltpu.VMEM)
    free = pl.BlockSpec(memory_space=pl.ANY)
    return pl.pallas_call(
        functools.partial(spread_kernel, count, heads),
        out_shape=(
            jax.ShapeDtypeStruct((2, 2) + key_raw.shape, jnp.bfloat16),
            jax.ShapeDtypeStruct((LOW, yn, ZN, 2 * G_DEV, width), jnp.bfloat16),
            jax.ShapeDtypeStruct(lines, jnp.float32),
            jax.ShapeDtypeStruct((2,) + lines, jnp.float32),
            jax.ShapeDtypeStruct((2, width), jnp.float32),
        ),
        in_specs=[pl.BlockSpec(memory_space=pltpu.SMEM), vmem, vmem, vmem, vmem, vmem],
        out_specs=(free, free, vmem, vmem, vmem),
        scratch_shapes=[
            pltpu.VMEM(lines, jnp.float32),
            pltpu.VMEM((heads - 1,) + lines, jnp.float32),
            pltpu.VMEM(lines, jnp.float32),
            pltpu.VMEM((2,) + lines, jnp.float32),
            pltpu.VMEM((2 * G_DEV, width), jnp.bfloat16),
            pltpu.SemaphoreType.DMA((8,)),
            pltpu.SemaphoreType.DMA((8,)),
            pltpu.SemaphoreType.DMA((heads - 1,)),
            pltpu.SemaphoreType.DMA((heads - 1,)),
            pltpu.SemaphoreType.DMA((copies,)),
            pltpu.SemaphoreType.DMA((copies,)),
            pltpu.SemaphoreType.DMA,
        ],
        compiler_params=pltpu.CompilerParams(collective_id=1, has_side_effects=True),
    )(ids, query_raw, key_raw, values, query_gain, key_gain)


def collect_kernel(
    count, heads, ids_ref, prev_ref, next_ref, part_ref, dots_ref, key_ref, gain_ref,
    from_ref, sum_ref, tot_ref, near_ref, extra_ref,
    slots, half, yslots, quarter, zslot, hslots, total_buf, near_buf, extra_buf, eslots,
    wsend, wrecv, gsend, grecv, hsend, hrecv, esend, erecv,
):
    y, z, low, yn, other_z, y_peers, low_peers, after, before = places(count)
    peers = head_peers(heads)
    greet(peers + [after, before, other_z] + y_peers + low_peers)
    wsems, hsems, gsems, esems = (wsend, wrecv), (hsend, hrecv), (gsend, grecv), (esend, erecv)
    dotted = start_all(dots_ref, hslots, hsems, peers)
    sent = []
    for o, peer in enumerate(low_peers):
        copy = remote(part_ref.at[:, lax.rem(low + 1 + o, LOW)], slots.at[o], gsems, o, peer)
        copy.start()
        sent.append(copy)
    tokens = key_ref.shape[0]
    moved = [
        remote(next_ref, from_ref.at[0], wsems, 0, after),
        remote(prev_ref, from_ref.at[1], wsems, 1, before),
    ]
    for copy in moved:
        copy.start()
    total = add_arrivals(dots_ref[...], hslots, dotted)
    total_buf[...] = total
    tot_ref[...] = total
    near = [
        remote(total_buf, near_buf.at[0], wsems, 2, after),
        remote(total_buf, near_buf.at[1], wsems, 3, before),
    ]
    for copy in near:
        copy.start()
    raw = own_tokens(ids_ref, lax.axis_index("ctx") * tokens, key_ref, key_ref) * gain_ref[1:2]
    summed = add_arrivals(part_ref[:, low], slots, sent)
    each = ZN * G_DEV
    for row in range(yn):
        half[row, 0:each] = summed[0, row * each : (row + 1) * each]
        half[row, each : 2 * each] = summed[1, row * each : (row + 1) * each]
    ysent = []
    for o, peer in enumerate(y_peers):
        copy = remote(half.at[lax.rem(y + 1 + o, yn)], yslots.at[o], gsems, LOW - 1 + o, peer)
        copy.start()
        ysent.append(copy)
    row = add_arrivals(half[y], yslots, ysent)
    quarter[...] = row
    swap = remote(quarter, zslot, gsems, LOW - 1 + yn - 1, other_z)
    swap.start()
    swap.wait_recv()
    reduced = row + zslot[...]
    sum_ref[...] = reduced
    share = jnp.sum(reduced[0:each] * raw, axis=1, keepdims=True)
    extra = jnp.broadcast_to(jnp.concatenate([share, share]), extra_buf.shape)
    extra_buf[...] = extra
    extras = start_all(extra_buf, eslots, esems, peers)
    extra_ref[...] = add_arrivals(extra, eslots, extras)
    for copy in near:
        copy.wait()
    near_ref[...] = near_buf[...]
    for copy in moved:
        copy.wait()
    for copy in sent + ysent + [swap] + dotted + extras:
        copy.wait_send()


def collect(ids, to_prev, to_next, parts, dots, key_raw, gains):
    count = lax.axis_size("ctx")
    heads = lax.axis_size("head")
    yn = count // (LOW * ZN)
    width = parts.shape[-1]
    rows = 2 * ZN * G_DEV
    copies = LOW - 1 + yn
    vmem = pl.BlockSpec(memory_space=pltpu.VMEM)
    free = pl.BlockSpec(memory_space=pl.ANY)
    return pl.pallas_call(
        functools.partial(collect_kernel, count, heads),
        out_shape=(
            jax.ShapeDtypeStruct((2,) + to_prev.shape, jnp.bfloat16),
            jax.ShapeDtypeStruct((rows, width), jnp.float32),
            jax.ShapeDtypeStruct(dots.shape, jnp.float32),
            jax.ShapeDtypeStruct((2,) + dots.shape, jnp.float32),
            jax.ShapeDtypeStruct((rows, 128), jnp.float32),
        ),
        in_specs=[pl.BlockSpec(memory_space=pltpu.SMEM), free, free, vmem, vmem, vmem, vmem],
        out_specs=(free, vmem, vmem, vmem, vmem),
        scratch_shapes=[
            pltpu.VMEM((LOW - 1, 2) + parts.shape[2:], jnp.float32),
            pltpu.VMEM((yn, rows, width), jnp.float32),
            pltpu.VMEM((yn - 1, rows, width), jnp.float32),
            pltpu.VMEM((rows, width), jnp.float32),
            pltpu.VMEM((rows, width), jnp.float32),
            pltpu.VMEM((heads - 1,) + dots.shape, jnp.float32),
            pltpu.VMEM(dots.shape, jnp.float32),
            pltpu.VMEM((2,) + dots.shape, jnp.float32),
            pltpu.VMEM((rows, 128), jnp.float32),
            pltpu.VMEM((heads - 1, rows, 128), jnp.float32),
            pltpu.SemaphoreType.DMA((8,)),
            pltpu.SemaphoreType.DMA((8,)),
            pltpu.SemaphoreType.DMA((copies,)),
            pltpu.SemaphoreType.DMA((copies,)),
            pltpu.SemaphoreType.DMA((heads - 1,)),
            pltpu.SemaphoreType.DMA((heads - 1,)),
            pltpu.SemaphoreType.DMA((heads - 1,)),
            pltpu.SemaphoreType.DMA((heads - 1,)),
        ],
        compiler_params=pltpu.CompilerParams(collective_id=2, has_side_effects=True),
    )(ids, to_prev, to_next, parts, dots, key_raw, gains)


def attention_kernel(
    tiles_ref, readers_ref, tot_ref, near_ref, gain_ref,
    q_ref, g_ref, key_ref, val_ref, win_ref, glob_ref,
    dq_ref, prev_ref, next_ref, own_ref, dglob_ref, dots_ref,
    inverses, queries, keys, vals, dkeys, dvals, dot_sums, live_buf,
):
    tokens = q_ref.shape[0]
    span = KEYS * TILE
    factor = HEAD_DIM ** (-0.5)

    @pl.when(pl.program_id(0) == 0)
    def _():
        own = lax.rsqrt(tot_ref[...] / D + EPSILON)
        near = lax.rsqrt(near_ref[...] / D + EPSILON)
        lines = [own[0:1], own[1:2], near[0, 2:3], near[0, 3:4]]
        lines += [own[2:3], own[3:4], near[1, 2:3], near[1, 3:4]]
        for index, line in enumerate(lines):
            inverses[index * TILE : (index + 1) * TILE] = jnp.broadcast_to(line, (TILE, TILE)).T
        dot_sums[...] = jnp.zeros_like(dot_sums)
        devices = readers_ref.shape[1]
        globals_here = glob_ref.shape[1]
        owner = lax.broadcasted_iota(jnp.int32, (devices, globals_here), 0)
        place = lax.broadcasted_iota(jnp.int32, (devices, globals_here), 1) // G_DEV
        groups = devices // LOW
        match = (owner % LOW == place // groups) & (owner // LOW == place % groups)
        flags = jnp.broadcast_to((readers_ref[...] > 0).astype(jnp.float32), (8, devices))
        live_buf[...] = dot(
            flags.astype(jnp.bfloat16), match.astype(jnp.float32).astype(jnp.bfloat16), ROWS
        )

    qgain = gain_ref[0:1]
    kgain = gain_ref[1:2]
    first_tile = (lax.axis_index("ctx") - 1) * (tokens // TILE)
    last_start = 3 * (tokens // TILE) - KEYS
    query_rows = q_ref[...].astype(jnp.float32)
    queries[...] = (query_rows * inverses[0:tokens] * qgain).astype(jnp.bfloat16)
    blocks = [win_ref[0, 0], key_ref[...], win_ref[1, 0]]
    for index, block in enumerate(blocks):
        rows = slice(index * tokens, (index + 1) * tokens)
        scale = inverses[(index + 1) * tokens : (index + 2) * tokens]
        keys[rows] = (block.astype(jnp.float32) * scale * kgain).astype(jnp.bfloat16)
    vals[0:tokens] = win_ref[0, 1]
    vals[tokens : 2 * tokens] = val_ref[...]
    vals[2 * tokens :] = win_ref[1, 1]
    dkeys[...] = jnp.zeros_like(dkeys)
    dvals[...] = jnp.zeros_like(dvals)
    gkeys = glob_ref[0]
    gvals = glob_ref[1]
    live = live_buf[0:1] > 0
    gdk = 0.0
    gdv = 0.0
    for tile in range(tokens // TILE):
        rows = slice(tile * TILE, (tile + 1) * TILE)
        start = jnp.clip(tiles_ref[tile, 0] - first_tile, 0, last_start)
        window = pl.ds(pl.multiple_of(start * TILE, TILE), span)
        query = queries[rows]
        grad = g_ref[rows]
        wkeys = keys[window]
        wvals = vals[window]
        score_w = dot(query, wkeys, TURNED) * factor
        score_g = jnp.where(live, dot(query, gkeys, TURNED) * factor, -jnp.inf)
        largest = jnp.maximum(
            jnp.max(score_w, axis=1, keepdims=True), jnp.max(score_g, axis=1, keepdims=True)
        )
        exp_w = jnp.exp(score_w - largest)
        exp_g = jnp.exp(score_g - largest)
        inverse = 1.0 / (
            jnp.sum(exp_w, axis=1, keepdims=True) + jnp.sum(exp_g, axis=1, keepdims=True)
        )
        prob_w = exp_w * inverse
        prob_g = exp_g * inverse
        low_w = prob_w.astype(jnp.bfloat16)
        low_g = prob_g.astype(jnp.bfloat16)
        attended = (dot(low_w, wvals, ROWS) + dot(low_g, gvals, ROWS)).astype(jnp.bfloat16)
        delta = jnp.sum(
            grad.astype(jnp.float32) * attended.astype(jnp.float32), axis=1, keepdims=True
        )
        ds_w = (prob_w * (dot(grad, wvals, TURNED) - delta) * factor).astype(jnp.bfloat16)
        ds_g = (prob_g * (dot(grad, gvals, TURNED) - delta) * factor).astype(jnp.bfloat16)
        dq_ref[rows] = dot(ds_w, wkeys, ROWS) + dot(ds_g, gkeys, ROWS)
        dkeys[window] += dot(ds_w, query, DOWN)
        dvals[window] += dot(low_w, grad, DOWN)
        gdk = gdk + dot(ds_g, query, DOWN)
        gdv = gdv + dot(low_g, grad, DOWN)
    for pair_index, cat in enumerate((dkeys, dvals)):
        prev_ref[pair_index] = cat[0:tokens].astype(jnp.bfloat16)
        own_ref[pair_index] = cat[tokens : 2 * tokens]
        next_ref[pair_index] = cat[2 * tokens :].astype(jnp.bfloat16)
    dglob_ref[0] = gdk
    dglob_ref[1] = gdv
    dot_sums[0:tokens] += dq_ref[...] * qgain * query_rows
    for index, block in enumerate(blocks):
        rows = slice(index * tokens, (index + 1) * tokens)
        dot_sums[(index + 1) * tokens : (index + 2) * tokens] += (
            dkeys[rows] * kgain * block.astype(jnp.float32)
        )

    @pl.when(pl.program_id(0) == pl.num_programs(0) - 1)
    def _():
        for index in range(dots_ref.shape[0]):
            turned = dot_sums[index * TILE : (index + 1) * TILE].T
            dots_ref[index : index + 1] = jnp.sum(turned, axis=0, keepdims=True)


def attention(tiles, readers, totals, near, gains, query, out_grad, key, val, window, globs):
    tokens, width = query.shape
    count = globs.shape[1]
    whole = pl.BlockSpec(memory_space=pltpu.VMEM)
    flat = pl.BlockSpec((tokens, HEAD_DIM), lambda h: (0, h))
    gain = pl.BlockSpec((2, HEAD_DIM), lambda h: (0, h))
    pair = pl.BlockSpec((2, tokens, HEAD_DIM), lambda h: (0, 0, h))
    glob = pl.BlockSpec((2, count, HEAD_DIM), lambda h: (0, 0, h))
    pair_shape = (2, tokens, width)
    lines = 4 * tokens // TILE
    return pl.pallas_call(
        attention_kernel,
        grid=(width // HEAD_DIM,),
        out_shape=(
            jax.ShapeDtypeStruct((tokens, width), jnp.float32),
            jax.ShapeDtypeStruct(pair_shape, jnp.bfloat16),
            jax.ShapeDtypeStruct(pair_shape, jnp.bfloat16),
            jax.ShapeDtypeStruct(pair_shape, jnp.float32),
            jax.ShapeDtypeStruct((2, count, width), jnp.float32),
            jax.ShapeDtypeStruct((lines, TILE), jnp.float32),
        ),
        in_specs=[
            pl.BlockSpec(memory_space=pltpu.SMEM),
            whole,
            whole,
            whole,
            gain,
            flat,
            flat,
            flat,
            flat,
            pl.BlockSpec((2, 2, tokens, HEAD_DIM), lambda h: (0, 0, 0, h)),
            glob,
        ],
        out_specs=(flat, pair, pair, pair, glob, pl.BlockSpec((lines, TILE), lambda h: (0, 0))),
        scratch_shapes=[
            pltpu.VMEM((4 * tokens, HEAD_DIM), jnp.float32),
            pltpu.VMEM((tokens, HEAD_DIM), jnp.bfloat16),
            pltpu.VMEM((3 * tokens, HEAD_DIM), jnp.bfloat16),
            pltpu.VMEM((3 * tokens, HEAD_DIM), jnp.bfloat16),
            pltpu.VMEM((3 * tokens, HEAD_DIM), jnp.float32),
            pltpu.VMEM((3 * tokens, HEAD_DIM), jnp.float32),
            pltpu.VMEM((4 * tokens, HEAD_DIM), jnp.float32),
            pltpu.VMEM((8, count), jnp.float32),
        ],
    )(tiles, readers, totals, near, gains, query, out_grad, key, val, window, globs)


def finish_kernel(
    ids_ref, tot_ref, sum_ref, dots_ref, near_ref, extra_ref, gain_ref,
    q_ref, k_ref, dq_ref, own_ref, from_ref, qg_ref, kg_ref, vg_ref, lines,
):
    tokens = q_ref.shape[0]
    device = lax.axis_index("ctx")
    z = lax.rem(device // LOW, ZN)
    spots = lax.broadcasted_iota(jnp.int32, (tokens, HEAD_DIM), 0) + device * tokens

    @pl.when(pl.program_id(0) == 0)
    def _():
        inverse = lax.rsqrt(tot_ref[...] / D + EPSILON)
        dots = dots_ref[...]
        key_dots = dots[4:6] + near_ref[0, 6:8] + near_ref[1, 2:4]
        rows = [inverse[0:1], inverse[1:2], inverse[2:3], inverse[3:4]]
        rows += [dots[0:1], dots[1:2], key_dots[0:1], key_dots[1:2]]
        for index, row in enumerate(rows):
            lines[index * TILE : (index + 1) * TILE] = jnp.broadcast_to(row, (TILE, TILE)).T
        for index in range(G_DEV):
            extra = jnp.where(z == 0, extra_ref[index : index + 1], extra_ref[G_DEV + index : G_DEV + index + 1])
            lines[3 * tokens :] += jnp.where(spots == ids_ref[index], extra, 0.0)

    home_key = own_ref[0] + from_ref[0, 0].astype(jnp.float32) + from_ref[1, 0].astype(jnp.float32)
    home_val = own_ref[1] + from_ref[0, 1].astype(jnp.float32) + from_ref[1, 1].astype(jnp.float32)
    each = ZN * G_DEV
    for index in range(G_DEV):
        here = spots == ids_ref[index]
        other = G_DEV + index
        add_key = jnp.where(z == 0, sum_ref[index : index + 1], sum_ref[other : other + 1])
        add_val = jnp.where(
            z == 0, sum_ref[each + index : each + index + 1], sum_ref[each + other : each + other + 1]
        )
        home_key = home_key + jnp.where(here, add_key, 0.0)
        home_val = home_val + jnp.where(here, add_val, 0.0)
    query_inv = lines[0:tokens]
    key_inv = lines[tokens : 2 * tokens]
    query_dot = lines[2 * tokens : 3 * tokens]
    key_dot = lines[3 * tokens :]
    qg_ref[...] = (
        query_inv * (gain_ref[0:1] * dq_ref[...])
        - q_ref[...].astype(jnp.float32) * (query_inv * query_inv * query_inv) * (query_dot / D)
    ).astype(jnp.bfloat16)
    kg_ref[...] = (
        key_inv * (gain_ref[1:2] * home_key)
        - k_ref[...].astype(jnp.float32) * (key_inv * key_inv * key_inv) * (key_dot / D)
    ).astype(jnp.bfloat16)
    vg_ref[...] = home_val.astype(jnp.bfloat16)


def finish(ids, totals, reduced, dots, near, extra, gains, query, key, dq, own, arrived):
    tokens, width = query.shape
    whole = pl.BlockSpec(memory_space=pltpu.VMEM)
    flat = pl.BlockSpec((tokens, HEAD_DIM), lambda h: (0, h))

    def rows(count):
        return pl.BlockSpec((count, HEAD_DIM), lambda h: (0, h))

    return pl.pallas_call(
        finish_kernel,
        grid=(width // HEAD_DIM,),
        out_shape=(jax.ShapeDtypeStruct((tokens, width), jnp.bfloat16),) * 3,
        in_specs=[
            pl.BlockSpec(memory_space=pltpu.SMEM),
            whole,
            rows(reduced.shape[0]),
            whole,
            whole,
            whole,
            rows(2),
            flat,
            flat,
            flat,
            pl.BlockSpec((2, tokens, HEAD_DIM), lambda h: (0, 0, h)),
            pl.BlockSpec((2, 2, tokens, HEAD_DIM), lambda h: (0, 0, 0, h)),
        ],
        out_specs=(flat,) * 3,
        scratch_shapes=[pltpu.VMEM((4 * tokens, HEAD_DIM), jnp.float32)],
    )(ids, totals, reduced, dots, near, extra, gains, query, key, dq, own, arrived)


def body(
    query_raw, key_raw, values, out_grad, query_gain, key_gain, key_tiles, global_ids, readers
):
    width = query_raw.shape[1]
    count = lax.axis_size("ctx")
    window, globs, totals, near, gains = spread(
        global_ids, query_raw, key_raw, values, query_gain, key_gain
    )
    globs = (
        globs.reshape(count, 2, G_DEV, width).transpose(1, 0, 2, 3).reshape(2, count * G_DEV, width)
    )
    grad_query, to_prev, to_next, own_grads, glob_grads, dots = attention(
        key_tiles, readers, totals, near, gains, query_raw, out_grad, key_raw, values, window, globs
    )
    parts = glob_grads.reshape(2, LOW, -1, width)
    arrived, reduced, dot_totals, dot_near, extra = collect(
        global_ids, to_prev, to_next, parts, dots, key_raw, gains
    )
    return tuple(finish(
        global_ids, totals, reduced, dot_totals, dot_near, extra, gains,
        query_raw, key_raw, grad_query, own_grads, arrived,
    ))


def solution(mesh):
    return jax.shard_map(
        body,
        mesh=mesh,
        in_specs=(
            P("ctx", "head"),
            P("ctx", "head"),
            P("ctx", "head"),
            P("ctx", "head"),
            P("head"),
            P("head"),
            P("ctx", None),
            P("ctx"),
            P("ctx", None),
        ),
        out_specs=(P("ctx", "head"), P("ctx", "head"), P("ctx", "head")),
        check_vma=False,
    )
```

```python
import functools

import jax
import jax.numpy as jnp
from jax import lax
from jax.experimental import pallas as pl
from jax.experimental.pallas import tpu as pltpu
from jax.sharding import PartitionSpec as P

HEAD_DIM = 128
D = 5120
TILE = 128
KEYS = 4
G_DEV = 2
MESH = pl.DeviceIdType.MESH

LOW = 8
ZN = 2

EPSILON = 1e-06


def dot(a, b, dims):
    return lax.dot_general(a, b, (dims, ((), ())), preferred_element_type=jnp.float32)


ROWS = ((1,), (0,))
TURNED = ((1,), (1,))
DOWN = ((0,), (0,))


def greet(targets):
    barrier = pltpu.get_barrier_semaphore()
    for target in targets:
        pl.semaphore_signal(barrier, inc=1, device_id=target, device_id_type=MESH)
    pl.semaphore_wait(barrier, len(targets))


def remote(src, dst, sems, index, target):
    return pltpu.make_async_remote_copy(
        src_ref=src,
        dst_ref=dst,
        send_sem=sems[0].at[index],
        recv_sem=sems[1].at[index],
        device_id=target,
        device_id_type=MESH,
    )


def head_peers(heads):
    me = lax.axis_index("head")
    return [{"head": lax.rem(me + o, heads)} for o in range(1, heads)]


def start_all(src, slots, sems, peers):
    copies = [remote(src, slots.at[o], sems, o, peer) for o, peer in enumerate(peers)]
    for copy in copies:
        copy.start()
    return copies


def add_arrivals(total, slots, copies):
    for o, copy in enumerate(copies):
        copy.wait_recv()
        total = total + slots[o].astype(jnp.float32)
    return total


def places(count):
    me = lax.axis_index("ctx")
    yn = count // (LOW * ZN)
    low = lax.rem(me, LOW)
    z = lax.rem(me // LOW, ZN)
    y = me // (LOW * ZN)

    def at(y, z, low):
        return {"ctx": (y * ZN + z) * LOW + low}

    other_z = at(y, 1 - z, low)
    y_peers = [at(lax.rem(y + o, yn), z, low) for o in range(1, yn)]
    low_peers = [at(y, z, lax.rem(low + o, LOW)) for o in range(1, LOW)]
    after = {"ctx": lax.rem(me + 1, count)}
    before = {"ctx": lax.rem(me + count - 1, count)}
    return y, z, low, yn, other_z, y_peers, low_peers, after, before


def own_tokens(ids_ref, first, key_ref, val_ref):
    tokens = key_ref.shape[0]
    rows = lax.broadcasted_iota(jnp.int32, (8, tokens), 0)
    spots = lax.broadcasted_iota(jnp.int32, (8, tokens), 1)
    picks = jnp.zeros((8, tokens), jnp.float32)
    for index in range(G_DEV):
        hit = (rows % G_DEV == index) & (spots == ids_ref[index] - first)
        picks = jnp.where(hit, 1.0, picks)
    picks = picks.astype(jnp.bfloat16)
    keys = dot(picks, key_ref[...], ROWS)[0:4]
    vals = dot(picks, val_ref[...], ROWS)[0:4]
    is_key = lax.broadcasted_iota(jnp.int32, keys.shape, 0) < G_DEV
    return jnp.where(is_key, keys, vals)


def spread_kernel(
    count, heads, ids_ref, query_ref, key_ref, val_ref, qgain_ref, kgain_ref,
    win_ref, glob_ref, tot_ref, near_ref, gain_ref,
    sq_buf, hslots, total_buf, near_buf, own_buf, wsend, wrecv, hsend, hrecv, gsend, grecv, lsem,
):
    y, z, low, yn, other_z, y_peers, low_peers, after, before = places(count)
    peers = head_peers(heads)
    greet(peers + [after, before, other_z] + y_peers + low_peers)
    wsems, hsems, gsems = (wsend, wrecv), (hsend, hrecv), (gsend, grecv)
    tokens, width = key_ref.shape
    early = pl.ds(0, TILE // 2)
    rest = pl.ds(TILE // 2, tokens - TILE // 2)
    moved = [
        remote(key_ref.at[early], win_ref.at[0, 0, early], wsems, 0, after),
        remote(key_ref.at[early], win_ref.at[1, 0, early], wsems, 1, before),
        remote(key_ref.at[rest], win_ref.at[0, 0, rest], wsems, 2, after),
        remote(key_ref.at[rest], win_ref.at[1, 0, rest], wsems, 3, before),
        remote(val_ref, win_ref.at[0, 1], wsems, 4, after),
        remote(val_ref, win_ref.at[1, 1], wsems, 5, before),
    ]
    for copy in moved[:2]:
        copy.start()
    first = lax.axis_index("ctx") * tokens
    line = 0
    for ref in (query_ref, key_ref):
        for start in range(0, tokens, TILE):
            folded = jnp.zeros((TILE, TILE), jnp.float32)
            for column in range(0, width, TILE):
                block = ref[start : start + TILE, column : column + TILE].astype(jnp.float32)
                folded = folded + block * block
            sq_buf[line : line + 1] = jnp.sum(folded.T, axis=0, keepdims=True)
            line += 1
    kgain = kgain_ref[...].reshape(1, width)
    gain_ref[0:1] = qgain_ref[...].reshape(1, width)
    gain_ref[1:2] = kgain
    raw = own_tokens(ids_ref, first, key_ref, val_ref)
    own_squares = jnp.sum(raw * raw, axis=1, keepdims=True)
    sq_buf[4:8] = jnp.broadcast_to(own_squares, (4, TILE))
    squares = sq_buf[...]
    summed = start_all(sq_buf, hslots, hsems, peers)
    total = add_arrivals(squares, hslots, summed)
    total_buf[...] = total
    tot_ref[...] = total
    inverse = lax.rsqrt(total[4:8, 0:1] / D + EPSILON)
    is_key = lax.broadcasted_iota(jnp.int32, raw.shape, 0) < G_DEV
    own_buf[...] = jnp.where(is_key, raw * inverse * kgain, raw).astype(jnp.bfloat16)
    swap = remote(own_buf, glob_ref.at[low, y, z], gsems, 0, other_z)
    swap.start()
    local = pltpu.make_async_copy(own_buf, glob_ref.at[low, y, z], lsem)
    local.start()
    near = [
        remote(total_buf, near_buf.at[0], wsems, 6, after),
        remote(total_buf, near_buf.at[1], wsems, 7, before),
    ]
    for copy in near + moved[2:]:
        copy.start()
    local.wait()
    remote(own_buf, glob_ref.at[low, y, 1 - z], gsems, 0, other_z).wait_recv()
    sent = [swap]
    for o, peer in enumerate(y_peers):
        copy = remote(glob_ref.at[low, y], glob_ref.at[low, y], gsems, 1 + o, peer)
        copy.start()
        sent.append(copy)
    for o, peer in enumerate(y_peers):
        source = lax.rem(y + yn - 1 - o, yn)
        remote(glob_ref.at[low, source], glob_ref.at[low, source], gsems, 1 + o, peer).wait_recv()
    for o, peer in enumerate(low_peers):
        copy = remote(glob_ref.at[low], glob_ref.at[low], gsems, yn + o, peer)
        copy.start()
        sent.append(copy)
    for o, peer in enumerate(low_peers):
        source = lax.rem(low + LOW - 1 - o, LOW)
        remote(glob_ref.at[source], glob_ref.at[source], gsems, yn + o, peer).wait_recv()
    for copy in near:
        copy.wait()
    near_ref[...] = near_buf[...]
    for copy in moved:
        copy.wait()
    for copy in sent + summed:
        copy.wait_send()


def spread(ids, query_raw, key_raw, values, query_gain, key_gain):
    count = lax.axis_size("ctx")
    heads = lax.axis_size("head")
    yn = count // (LOW * ZN)
    width = key_raw.shape[-1]
    lines = (8, TILE)
    copies = yn + LOW - 1
    vmem = pl.BlockSpec(memory_space=pltpu.VMEM)
    free = pl.BlockSpec(memory_space=pl.ANY)
    return pl.pallas_call(
        functools.partial(spread_kernel, count, heads),
        out_shape=(
            jax.ShapeDtypeStruct((2, 2) + key_raw.shape, jnp.bfloat16),
            jax.ShapeDtypeStruct((LOW, yn, ZN, 2 * G_DEV, width), jnp.bfloat16),
            jax.ShapeDtypeStruct(lines, jnp.float32),
            jax.ShapeDtypeStruct((2,) + lines, jnp.float32),
            jax.ShapeDtypeStruct((2, width), jnp.float32),
        ),
        in_specs=[pl.BlockSpec(memory_space=pltpu.SMEM), vmem, vmem, vmem, vmem, vmem],
        out_specs=(free, free, vmem, vmem, vmem),
        scratch_shapes=[
            pltpu.VMEM(lines, jnp.float32),
            pltpu.VMEM((heads - 1,) + lines, jnp.float32),
            pltpu.VMEM(lines, jnp.float32),
            pltpu.VMEM((2,) + lines, jnp.float32),
            pltpu.VMEM((2 * G_DEV, width), jnp.bfloat16),
            pltpu.SemaphoreType.DMA((8,)),
            pltpu.SemaphoreType.DMA((8,)),
            pltpu.SemaphoreType.DMA((heads - 1,)),
            pltpu.SemaphoreType.DMA((heads - 1,)),
            pltpu.SemaphoreType.DMA((copies,)),
            pltpu.SemaphoreType.DMA((copies,)),
            pltpu.SemaphoreType.DMA,
        ],
        compiler_params=pltpu.CompilerParams(collective_id=1, has_side_effects=True),
    )(ids, query_raw, key_raw, values, query_gain, key_gain)


def collect_kernel(
    count, heads, ids_ref, prev_ref, next_ref, part_ref, dots_ref, key_ref, gain_ref,
    from_ref, sum_ref, tot_ref, near_ref, extra_ref,
    slots, half, yslots, quarter, zslot, hslots, total_buf, near_buf, extra_buf, eslots,
    wsend, wrecv, gsend, grecv, hsend, hrecv, esend, erecv,
):
    y, z, low, yn, other_z, y_peers, low_peers, after, before = places(count)
    peers = head_peers(heads)
    greet(peers + [after, before, other_z] + y_peers + low_peers)
    wsems, hsems, gsems, esems = (wsend, wrecv), (hsend, hrecv), (gsend, grecv), (esend, erecv)
    dotted = start_all(dots_ref, hslots, hsems, peers)
    sent = []
    for o, peer in enumerate(low_peers):
        copy = remote(part_ref.at[:, lax.rem(low + 1 + o, LOW)], slots.at[o], gsems, o, peer)
        copy.start()
        sent.append(copy)
    tokens = key_ref.shape[0]
    upper = pl.ds(0, TILE)
    lower = pl.ds(TILE, tokens - TILE)
    moved = [
        remote(next_ref.at[0], from_ref.at[0, 0], wsems, 0, after),
        remote(prev_ref.at[0], from_ref.at[1, 0], wsems, 1, before),
        remote(next_ref.at[1, upper], from_ref.at[0, 1, upper], wsems, 4, after),
        remote(prev_ref.at[1, upper], from_ref.at[1, 1, upper], wsems, 5, before),
        remote(next_ref.at[1, lower], from_ref.at[0, 1, lower], wsems, 6, after),
        remote(prev_ref.at[1, lower], from_ref.at[1, 1, lower], wsems, 7, before),
    ]
    for copy in moved[:2]:
        copy.start()
    total = add_arrivals(dots_ref[...], hslots, dotted)
    total_buf[...] = total
    tot_ref[...] = total
    near = [
        remote(total_buf, near_buf.at[0], wsems, 2, after),
        remote(total_buf, near_buf.at[1], wsems, 3, before),
    ]
    for copy in near:
        copy.start()
    raw = own_tokens(ids_ref, lax.axis_index("ctx") * tokens, key_ref, key_ref) * gain_ref[1:2]
    summed = add_arrivals(part_ref[:, low].astype(jnp.float32), slots, sent)
    each = ZN * G_DEV
    for row in range(yn):
        half[row, 0:each] = summed[0, row * each : (row + 1) * each]
        half[row, each : 2 * each] = summed[1, row * each : (row + 1) * each]
    ysent = []
    for o, peer in enumerate(y_peers):
        copy = remote(half.at[lax.rem(y + 1 + o, yn)], yslots.at[o], gsems, LOW - 1 + o, peer)
        copy.start()
        ysent.append(copy)
    row = add_arrivals(half[y], yslots, ysent)
    quarter[...] = row
    swap = remote(quarter, zslot, gsems, LOW - 1 + yn - 1, other_z)
    for copy in [swap] + moved[2:4]:
        copy.start()
    swap.wait_recv()
    reduced = row + zslot[...]
    sum_ref[...] = reduced
    share = jnp.sum(reduced[0:each] * raw, axis=1, keepdims=True)
    extra = jnp.broadcast_to(jnp.concatenate([share, share]), extra_buf.shape)
    extra_buf[...] = extra
    extras = start_all(extra_buf, eslots, esems, peers)
    for copy in moved[4:]:
        copy.start()
    extra_ref[...] = add_arrivals(extra, eslots, extras)
    for copy in near:
        copy.wait()
    near_ref[...] = near_buf[...]
    for copy in moved:
        copy.wait()
    for copy in sent + ysent + [swap] + dotted + extras:
        copy.wait_send()


def collect(ids, to_prev, to_next, parts, dots, key_raw, gains):
    count = lax.axis_size("ctx")
    heads = lax.axis_size("head")
    yn = count // (LOW * ZN)
    width = parts.shape[-1]
    rows = 2 * ZN * G_DEV
    copies = LOW - 1 + yn
    vmem = pl.BlockSpec(memory_space=pltpu.VMEM)
    free = pl.BlockSpec(memory_space=pl.ANY)
    return pl.pallas_call(
        functools.partial(collect_kernel, count, heads),
        out_shape=(
            jax.ShapeDtypeStruct((2,) + to_prev.shape, jnp.bfloat16),
            jax.ShapeDtypeStruct((rows, width), jnp.float32),
            jax.ShapeDtypeStruct(dots.shape, jnp.float32),
            jax.ShapeDtypeStruct((2,) + dots.shape, jnp.float32),
            jax.ShapeDtypeStruct((rows, 128), jnp.float32),
        ),
        in_specs=[pl.BlockSpec(memory_space=pltpu.SMEM), free, free, vmem, vmem, vmem, vmem],
        out_specs=(free, vmem, vmem, vmem, vmem),
        scratch_shapes=[
            pltpu.VMEM((LOW - 1, 2) + parts.shape[2:], jnp.bfloat16),
            pltpu.VMEM((yn, rows, width), jnp.float32),
            pltpu.VMEM((yn - 1, rows, width), jnp.float32),
            pltpu.VMEM((rows, width), jnp.float32),
            pltpu.VMEM((rows, width), jnp.float32),
            pltpu.VMEM((heads - 1,) + dots.shape, jnp.float32),
            pltpu.VMEM(dots.shape, jnp.float32),
            pltpu.VMEM((2,) + dots.shape, jnp.float32),
            pltpu.VMEM((rows, 128), jnp.float32),
            pltpu.VMEM((heads - 1, rows, 128), jnp.float32),
            pltpu.SemaphoreType.DMA((8,)),
            pltpu.SemaphoreType.DMA((8,)),
            pltpu.SemaphoreType.DMA((copies,)),
            pltpu.SemaphoreType.DMA((copies,)),
            pltpu.SemaphoreType.DMA((heads - 1,)),
            pltpu.SemaphoreType.DMA((heads - 1,)),
            pltpu.SemaphoreType.DMA((heads - 1,)),
            pltpu.SemaphoreType.DMA((heads - 1,)),
        ],
        compiler_params=pltpu.CompilerParams(collective_id=2, has_side_effects=True),
    )(ids, to_prev, to_next, parts, dots, key_raw, gains)


def attention_kernel(
    tiles_ref, readers_ref, tot_ref, near_ref, gain_ref,
    q_ref, g_ref, key_ref, val_ref, win_ref, glob_ref,
    dq_ref, prev_ref, next_ref, own_ref, dglob_ref, dots_ref,
    inverses, queries, keys, vals, dkeys, dvals, dot_sums, live_buf,
):
    tokens = q_ref.shape[0]
    span = KEYS * TILE
    factor = HEAD_DIM ** (-0.5)

    @pl.when(pl.program_id(0) == 0)
    def _():
        own = lax.rsqrt(tot_ref[...] / D + EPSILON)
        near = lax.rsqrt(near_ref[...] / D + EPSILON)
        lines = [own[0:1], own[1:2], near[0, 2:3], near[0, 3:4]]
        lines += [own[2:3], own[3:4], near[1, 2:3], near[1, 3:4]]
        for index, line in enumerate(lines):
            inverses[index * TILE : (index + 1) * TILE] = jnp.broadcast_to(line, (TILE, TILE)).T
        dot_sums[...] = jnp.zeros_like(dot_sums)
        devices = readers_ref.shape[1]
        globals_here = glob_ref.shape[1]
        owner = lax.broadcasted_iota(jnp.int32, (devices, globals_here), 0)
        place = lax.broadcasted_iota(jnp.int32, (devices, globals_here), 1) // G_DEV
        groups = devices // LOW
        match = (owner % LOW == place // groups) & (owner // LOW == place % groups)
        flags = jnp.broadcast_to((readers_ref[...] > 0).astype(jnp.float32), (8, devices))
        live_buf[...] = dot(
            flags.astype(jnp.bfloat16), match.astype(jnp.float32).astype(jnp.bfloat16), ROWS
        )

    qgain = gain_ref[0:1]
    kgain = gain_ref[1:2]
    first_tile = (lax.axis_index("ctx") - 1) * (tokens // TILE)
    last_start = 3 * (tokens // TILE) - KEYS
    query_rows = q_ref[...].astype(jnp.float32)
    queries[...] = (query_rows * inverses[0:tokens] * qgain).astype(jnp.bfloat16)
    blocks = [win_ref[0, 0], key_ref[...], win_ref[1, 0]]
    for index, block in enumerate(blocks):
        rows = slice(index * tokens, (index + 1) * tokens)
        scale = inverses[(index + 1) * tokens : (index + 2) * tokens]
        keys[rows] = (block.astype(jnp.float32) * scale * kgain).astype(jnp.bfloat16)
    vals[0:tokens] = win_ref[0, 1]
    vals[tokens : 2 * tokens] = val_ref[...]
    vals[2 * tokens :] = win_ref[1, 1]
    dkeys[...] = jnp.zeros_like(dkeys)
    dvals[...] = jnp.zeros_like(dvals)
    gkeys = glob_ref[0]
    gvals = glob_ref[1]
    live = live_buf[0:1] > 0
    gdk = 0.0
    gdv = 0.0
    for tile in range(tokens // TILE):
        rows = slice(tile * TILE, (tile + 1) * TILE)
        start = jnp.clip(tiles_ref[tile, 0] - first_tile, 0, last_start)
        window = pl.ds(pl.multiple_of(start * TILE, TILE), span)
        query = queries[rows]
        grad = g_ref[rows]
        wkeys = keys[window]
        wvals = vals[window]
        score_w = dot(query, wkeys, TURNED) * factor
        score_g = jnp.where(live, dot(query, gkeys, TURNED) * factor, -jnp.inf)
        largest = jnp.maximum(
            jnp.max(score_w, axis=1, keepdims=True), jnp.max(score_g, axis=1, keepdims=True)
        )
        exp_w = jnp.exp(score_w - largest)
        exp_g = jnp.exp(score_g - largest)
        inverse = 1.0 / (
            jnp.sum(exp_w, axis=1, keepdims=True) + jnp.sum(exp_g, axis=1, keepdims=True)
        )
        prob_w = exp_w * inverse
        prob_g = exp_g * inverse
        low_w = prob_w.astype(jnp.bfloat16)
        low_g = prob_g.astype(jnp.bfloat16)
        attended = (dot(low_w, wvals, ROWS) + dot(low_g, gvals, ROWS)).astype(jnp.bfloat16)
        delta = jnp.sum(
            grad.astype(jnp.float32) * attended.astype(jnp.float32), axis=1, keepdims=True
        )
        ds_w = (prob_w * (dot(grad, wvals, TURNED) - delta) * factor).astype(jnp.bfloat16)
        ds_g = (prob_g * (dot(grad, gvals, TURNED) - delta) * factor).astype(jnp.bfloat16)
        dq_ref[rows] = dot(ds_w, wkeys, ROWS) + dot(ds_g, gkeys, ROWS)
        dkeys[window] += dot(ds_w, query, DOWN)
        dvals[window] += dot(low_w, grad, DOWN)
        gdk = gdk + dot(ds_g, query, DOWN)
        gdv = gdv + dot(low_g, grad, DOWN)
    for pair_index, cat in enumerate((dkeys, dvals)):
        prev_ref[pair_index] = cat[0:tokens].astype(jnp.bfloat16)
        own_ref[pair_index] = cat[tokens : 2 * tokens]
        next_ref[pair_index] = cat[2 * tokens :].astype(jnp.bfloat16)
    dglob_ref[0] = gdk.astype(jnp.bfloat16)
    dglob_ref[1] = gdv.astype(jnp.bfloat16)
    dot_sums[0:tokens] += dq_ref[...] * qgain * query_rows
    for index, block in enumerate(blocks):
        rows = slice(index * tokens, (index + 1) * tokens)
        dot_sums[(index + 1) * tokens : (index + 2) * tokens] += (
            dkeys[rows] * kgain * block.astype(jnp.float32)
        )

    @pl.when(pl.program_id(0) == pl.num_programs(0) - 1)
    def _():
        for index in range(dots_ref.shape[0]):
            turned = dot_sums[index * TILE : (index + 1) * TILE].T
            dots_ref[index : index + 1] = jnp.sum(turned, axis=0, keepdims=True)


def attention(tiles, readers, totals, near, gains, query, out_grad, key, val, window, globs):
    tokens, width = query.shape
    count = globs.shape[1]
    whole = pl.BlockSpec(memory_space=pltpu.VMEM)
    flat = pl.BlockSpec((tokens, HEAD_DIM), lambda h: (0, h))
    gain = pl.BlockSpec((2, HEAD_DIM), lambda h: (0, h))
    pair = pl.BlockSpec((2, tokens, HEAD_DIM), lambda h: (0, 0, h))
    glob = pl.BlockSpec((2, count, HEAD_DIM), lambda h: (0, 0, h))
    pair_shape = (2, tokens, width)
    lines = 4 * tokens // TILE
    return pl.pallas_call(
        attention_kernel,
        grid=(width // HEAD_DIM,),
        out_shape=(
            jax.ShapeDtypeStruct((tokens, width), jnp.float32),
            jax.ShapeDtypeStruct(pair_shape, jnp.bfloat16),
            jax.ShapeDtypeStruct(pair_shape, jnp.bfloat16),
            jax.ShapeDtypeStruct(pair_shape, jnp.float32),
            jax.ShapeDtypeStruct((2, count, width), jnp.bfloat16),
            jax.ShapeDtypeStruct((lines, TILE), jnp.float32),
        ),
        in_specs=[
            pl.BlockSpec(memory_space=pltpu.SMEM),
            whole,
            whole,
            whole,
            gain,
            flat,
            flat,
            flat,
            flat,
            pl.BlockSpec((2, 2, tokens, HEAD_DIM), lambda h: (0, 0, 0, h)),
            glob,
        ],
        out_specs=(flat, pair, pair, pair, glob, pl.BlockSpec((lines, TILE), lambda h: (0, 0))),
        scratch_shapes=[
            pltpu.VMEM((4 * tokens, HEAD_DIM), jnp.float32),
            pltpu.VMEM((tokens, HEAD_DIM), jnp.bfloat16),
            pltpu.VMEM((3 * tokens, HEAD_DIM), jnp.bfloat16),
            pltpu.VMEM((3 * tokens, HEAD_DIM), jnp.bfloat16),
            pltpu.VMEM((3 * tokens, HEAD_DIM), jnp.float32),
            pltpu.VMEM((3 * tokens, HEAD_DIM), jnp.float32),
            pltpu.VMEM((4 * tokens, HEAD_DIM), jnp.float32),
            pltpu.VMEM((8, count), jnp.float32),
        ],
    )(tiles, readers, totals, near, gains, query, out_grad, key, val, window, globs)


def finish_kernel(
    ids_ref, tot_ref, sum_ref, dots_ref, near_ref, extra_ref, gain_ref,
    q_ref, k_ref, dq_ref, own_ref, from_ref, qg_ref, kg_ref, vg_ref, lines,
):
    tokens = q_ref.shape[0]
    device = lax.axis_index("ctx")
    z = lax.rem(device // LOW, ZN)
    spots = lax.broadcasted_iota(jnp.int32, (tokens, HEAD_DIM), 0) + device * tokens

    @pl.when(pl.program_id(0) == 0)
    def _():
        inverse = lax.rsqrt(tot_ref[...] / D + EPSILON)
        dots = dots_ref[...]
        key_dots = dots[4:6] + near_ref[0, 6:8] + near_ref[1, 2:4]
        rows = [inverse[0:1], inverse[1:2], inverse[2:3], inverse[3:4]]
        rows += [dots[0:1], dots[1:2], key_dots[0:1], key_dots[1:2]]
        for index, row in enumerate(rows):
            lines[index * TILE : (index + 1) * TILE] = jnp.broadcast_to(row, (TILE, TILE)).T
        for index in range(G_DEV):
            extra = jnp.where(z == 0, extra_ref[index : index + 1], extra_ref[G_DEV + index : G_DEV + index + 1])
            lines[3 * tokens :] += jnp.where(spots == ids_ref[index], extra, 0.0)

    home_key = own_ref[0] + from_ref[0, 0].astype(jnp.float32) + from_ref[1, 0].astype(jnp.float32)
    home_val = own_ref[1] + from_ref[0, 1].astype(jnp.float32) + from_ref[1, 1].astype(jnp.float32)
    each = ZN * G_DEV
    for index in range(G_DEV):
        here = spots == ids_ref[index]
        other = G_DEV + index
        add_key = jnp.where(z == 0, sum_ref[index : index + 1], sum_ref[other : other + 1])
        add_val = jnp.where(
            z == 0, sum_ref[each + index : each + index + 1], sum_ref[each + other : each + other + 1]
        )
        home_key = home_key + jnp.where(here, add_key, 0.0)
        home_val = home_val + jnp.where(here, add_val, 0.0)
    query_inv = lines[0:tokens]
    key_inv = lines[tokens : 2 * tokens]
    query_dot = lines[2 * tokens : 3 * tokens]
    key_dot = lines[3 * tokens :]
    qg_ref[...] = (
        query_inv * (gain_ref[0:1] * dq_ref[...])
        - q_ref[...].astype(jnp.float32) * (query_inv * query_inv * query_inv) * (query_dot / D)
    ).astype(jnp.bfloat16)
    kg_ref[...] = (
        key_inv * (gain_ref[1:2] * home_key)
        - k_ref[...].astype(jnp.float32) * (key_inv * key_inv * key_inv) * (key_dot / D)
    ).astype(jnp.bfloat16)
    vg_ref[...] = home_val.astype(jnp.bfloat16)


def finish(ids, totals, reduced, dots, near, extra, gains, query, key, dq, own, arrived):
    tokens, width = query.shape
    whole = pl.BlockSpec(memory_space=pltpu.VMEM)
    flat = pl.BlockSpec((tokens, HEAD_DIM), lambda h: (0, h))

    def rows(count):
        return pl.BlockSpec((count, HEAD_DIM), lambda h: (0, h))

    return pl.pallas_call(
        finish_kernel,
        grid=(width // HEAD_DIM,),
        out_shape=(jax.ShapeDtypeStruct((tokens, width), jnp.bfloat16),) * 3,
        in_specs=[
            pl.BlockSpec(memory_space=pltpu.SMEM),
            whole,
            rows(reduced.shape[0]),
            whole,
            whole,
            whole,
            rows(2),
            flat,
            flat,
            flat,
            pl.BlockSpec((2, tokens, HEAD_DIM), lambda h: (0, 0, h)),
            pl.BlockSpec((2, 2, tokens, HEAD_DIM), lambda h: (0, 0, 0, h)),
        ],
        out_specs=(flat,) * 3,
        scratch_shapes=[pltpu.VMEM((4 * tokens, HEAD_DIM), jnp.float32)],
    )(ids, totals, reduced, dots, near, extra, gains, query, key, dq, own, arrived)


def body(
    query_raw, key_raw, values, out_grad, query_gain, key_gain, key_tiles, global_ids, readers
):
    width = query_raw.shape[1]
    count = lax.axis_size("ctx")
    window, globs, totals, near, gains = spread(
        global_ids, query_raw, key_raw, values, query_gain, key_gain
    )
    globs = (
        globs.reshape(count, 2, G_DEV, width).transpose(1, 0, 2, 3).reshape(2, count * G_DEV, width)
    )
    grad_query, to_prev, to_next, own_grads, glob_grads, dots = attention(
        key_tiles, readers, totals, near, gains, query_raw, out_grad, key_raw, values, window, globs
    )
    parts = glob_grads.reshape(2, LOW, -1, width)
    arrived, reduced, dot_totals, dot_near, extra = collect(
        global_ids, to_prev, to_next, parts, dots, key_raw, gains
    )
    return tuple(finish(
        global_ids, totals, reduced, dot_totals, dot_near, extra, gains,
        query_raw, key_raw, grad_query, own_grads, arrived,
    ))


def solution(mesh):
    return jax.shard_map(
        body,
        mesh=mesh,
        in_specs=(
            P("ctx", "head"),
            P("ctx", "head"),
            P("ctx", "head"),
            P("ctx", "head"),
            P("head"),
            P("head"),
            P("ctx", None),
            P("ctx"),
            P("ctx", None),
        ),
        out_specs=(P("ctx", "head"), P("ctx", "head"), P("ctx", "head")),
        check_vma=False,
    )
```

```python
import functools

import jax
import jax.numpy as jnp
from jax import lax
from jax.experimental import pallas as pl
from jax.experimental.pallas import tpu as pltpu
from jax.sharding import PartitionSpec as P

HEAD_DIM = 128
D = 5120
TILE = 128
KEYS = 4
G_DEV = 2
MESH = pl.DeviceIdType.MESH

LOW = 8
ZN = 2

EPSILON = 1e-06


def dot(a, b, dims):
    return lax.dot_general(a, b, (dims, ((), ())), preferred_element_type=jnp.float32)


ROWS = ((1,), (0,))
TURNED = ((1,), (1,))
DOWN = ((0,), (0,))


def greet(targets):
    barrier = pltpu.get_barrier_semaphore()
    for target in targets:
        pl.semaphore_signal(barrier, inc=1, device_id=target, device_id_type=MESH)
    pl.semaphore_wait(barrier, len(targets))


def remote(src, dst, sems, index, target):
    return pltpu.make_async_remote_copy(
        src_ref=src,
        dst_ref=dst,
        send_sem=sems[0].at[index],
        recv_sem=sems[1].at[index],
        device_id=target,
        device_id_type=MESH,
    )


def head_peers(heads):
    me = lax.axis_index("head")
    return [{"head": lax.rem(me + o, heads)} for o in range(1, heads)]


def start_all(src, slots, sems, peers):
    copies = [remote(src, slots.at[o], sems, o, peer) for o, peer in enumerate(peers)]
    for copy in copies:
        copy.start()
    return copies


def add_arrivals(total, slots, copies):
    for o, copy in enumerate(copies):
        copy.wait_recv()
        total = total + slots[o].astype(jnp.float32)
    return total


def places(count):
    me = lax.axis_index("ctx")
    yn = count // (LOW * ZN)
    low = lax.rem(me, LOW)
    z = lax.rem(me // LOW, ZN)
    y = me // (LOW * ZN)

    def at(y, z, low):
        return {"ctx": (y * ZN + z) * LOW + low}

    other_z = at(y, 1 - z, low)
    y_peers = [at(lax.rem(y + o, yn), z, low) for o in range(1, yn)]
    low_peers = [at(y, z, lax.rem(low + o, LOW)) for o in range(1, LOW)]
    after = {"ctx": lax.rem(me + 1, count)}
    before = {"ctx": lax.rem(me + count - 1, count)}
    return y, z, low, yn, other_z, y_peers, low_peers, after, before


def own_tokens(ids_ref, first, key_ref, val_ref):
    tokens = key_ref.shape[0]
    rows = lax.broadcasted_iota(jnp.int32, (8, tokens), 0)
    spots = lax.broadcasted_iota(jnp.int32, (8, tokens), 1)
    picks = jnp.zeros((8, tokens), jnp.float32)
    for index in range(G_DEV):
        hit = (rows % G_DEV == index) & (spots == ids_ref[index] - first)
        picks = jnp.where(hit, 1.0, picks)
    picks = picks.astype(jnp.bfloat16)
    keys = dot(picks, key_ref[...], ROWS)[0:4]
    vals = dot(picks, val_ref[...], ROWS)[0:4]
    is_key = lax.broadcasted_iota(jnp.int32, keys.shape, 0) < G_DEV
    return jnp.where(is_key, keys, vals)


def spread_kernel(
    count, heads, ids_ref, query_ref, key_ref, val_ref, qgain_ref, kgain_ref,
    win_ref, glob_ref, tot_ref, near_ref, gain_ref,
    sq_buf, hslots, total_buf, near_buf, own_buf, wsend, wrecv, hsend, hrecv, gsend, grecv, lsem,
):
    y, z, low, yn, other_z, y_peers, low_peers, after, before = places(count)
    peers = head_peers(heads)
    greet(peers + [after, before, other_z] + y_peers + low_peers)
    wsems, hsems, gsems = (wsend, wrecv), (hsend, hrecv), (gsend, grecv)
    tokens, width = key_ref.shape
    early = pl.ds(0, TILE // 2)
    rest = pl.ds(TILE // 2, tokens - TILE // 2)
    moved = [
        remote(key_ref.at[early], win_ref.at[0, 0, early], wsems, 0, after),
        remote(key_ref.at[early], win_ref.at[1, 0, early], wsems, 1, before),
        remote(key_ref.at[rest], win_ref.at[0, 0, rest], wsems, 2, after),
        remote(key_ref.at[rest], win_ref.at[1, 0, rest], wsems, 3, before),
        remote(val_ref, win_ref.at[0, 1], wsems, 4, after),
        remote(val_ref, win_ref.at[1, 1], wsems, 5, before),
    ]
    for copy in moved[:2]:
        copy.start()
    first = lax.axis_index("ctx") * tokens
    line = 0
    for ref in (query_ref, key_ref):
        for start in range(0, tokens, TILE):
            folded = jnp.zeros((TILE, TILE), jnp.float32)
            for column in range(0, width, TILE):
                block = ref[start : start + TILE, column : column + TILE].astype(jnp.float32)
                folded = folded + block * block
            sq_buf[line : line + 1] = jnp.sum(folded.T, axis=0, keepdims=True)
            line += 1
    kgain = kgain_ref[...].reshape(1, width)
    gain_ref[0:1] = qgain_ref[...].reshape(1, width)
    gain_ref[1:2] = kgain
    raw = own_tokens(ids_ref, first, key_ref, val_ref)
    own_squares = jnp.sum(raw * raw, axis=1, keepdims=True)
    sq_buf[4:8] = jnp.broadcast_to(own_squares, (4, TILE))
    squares = sq_buf[...]
    summed = start_all(sq_buf, hslots, hsems, peers)
    total = add_arrivals(squares, hslots, summed)
    total_buf[...] = total
    tot_ref[...] = total
    inverse = lax.rsqrt(total[4:8, 0:1] / D + EPSILON)
    is_key = lax.broadcasted_iota(jnp.int32, raw.shape, 0) < G_DEV
    own_buf[...] = jnp.where(is_key, raw * inverse * kgain, raw).astype(jnp.bfloat16)
    swap = remote(own_buf, glob_ref.at[low, y, z], gsems, 0, other_z)
    swap.start()
    local = pltpu.make_async_copy(own_buf, glob_ref.at[low, y, z], lsem)
    local.start()
    near = [
        remote(total_buf, near_buf.at[0], wsems, 6, after),
        remote(total_buf, near_buf.at[1], wsems, 7, before),
    ]
    for copy in near + moved[2:]:
        copy.start()
    local.wait()
    remote(own_buf, glob_ref.at[low, y, 1 - z], gsems, 0, other_z).wait_recv()
    sent = [swap]
    for o, peer in enumerate(y_peers):
        copy = remote(glob_ref.at[low, y], glob_ref.at[low, y], gsems, 1 + o, peer)
        copy.start()
        sent.append(copy)
    for o, peer in enumerate(y_peers):
        source = lax.rem(y + yn - 1 - o, yn)
        remote(glob_ref.at[low, source], glob_ref.at[low, source], gsems, 1 + o, peer).wait_recv()
    for o, peer in enumerate(low_peers):
        copy = remote(glob_ref.at[low], glob_ref.at[low], gsems, yn + o, peer)
        copy.start()
        sent.append(copy)
    for o, peer in enumerate(low_peers):
        source = lax.rem(low + LOW - 1 - o, LOW)
        remote(glob_ref.at[source], glob_ref.at[source], gsems, yn + o, peer).wait_recv()
    for copy in near:
        copy.wait()
    near_ref[...] = near_buf[...]
    for copy in moved:
        copy.wait()
    for copy in sent + summed:
        copy.wait_send()


def spread(ids, query_raw, key_raw, values, query_gain, key_gain):
    count = lax.axis_size("ctx")
    heads = lax.axis_size("head")
    yn = count // (LOW * ZN)
    width = key_raw.shape[-1]
    lines = (8, TILE)
    copies = yn + LOW - 1
    vmem = pl.BlockSpec(memory_space=pltpu.VMEM)
    free = pl.BlockSpec(memory_space=pl.ANY)
    return pl.pallas_call(
        functools.partial(spread_kernel, count, heads),
        out_shape=(
            jax.ShapeDtypeStruct((2, 2) + key_raw.shape, jnp.bfloat16),
            jax.ShapeDtypeStruct((LOW, yn, ZN, 2 * G_DEV, width), jnp.bfloat16),
            jax.ShapeDtypeStruct(lines, jnp.float32),
            jax.ShapeDtypeStruct((2,) + lines, jnp.float32),
            jax.ShapeDtypeStruct((2, width), jnp.float32),
        ),
        in_specs=[pl.BlockSpec(memory_space=pltpu.SMEM), vmem, vmem, vmem, vmem, vmem],
        out_specs=(free, free, vmem, vmem, vmem),
        scratch_shapes=[
            pltpu.VMEM(lines, jnp.float32),
            pltpu.VMEM((heads - 1,) + lines, jnp.float32),
            pltpu.VMEM(lines, jnp.float32),
            pltpu.VMEM((2,) + lines, jnp.float32),
            pltpu.VMEM((2 * G_DEV, width), jnp.bfloat16),
            pltpu.SemaphoreType.DMA((8,)),
            pltpu.SemaphoreType.DMA((8,)),
            pltpu.SemaphoreType.DMA((heads - 1,)),
            pltpu.SemaphoreType.DMA((heads - 1,)),
            pltpu.SemaphoreType.DMA((copies,)),
            pltpu.SemaphoreType.DMA((copies,)),
            pltpu.SemaphoreType.DMA,
        ],
        compiler_params=pltpu.CompilerParams(collective_id=1, has_side_effects=True),
    )(ids, query_raw, key_raw, values, query_gain, key_gain)


def collect_kernel(
    count, heads, ids_ref, prev_ref, next_ref, part_ref, dots_ref, key_ref, gain_ref,
    from_ref, sum_ref, tot_ref, near_ref, extra_ref,
    slots, half, yslots, quarter, zslot, hslots, total_buf, near_buf, extra_buf, eslots,
    wsend, wrecv, gsend, grecv, hsend, hrecv, esend, erecv,
):
    y, z, low, yn, other_z, y_peers, low_peers, after, before = places(count)
    peers = head_peers(heads)
    greet(peers + [after, before, other_z] + y_peers + low_peers)
    wsems, hsems, gsems, esems = (wsend, wrecv), (hsend, hrecv), (gsend, grecv), (esend, erecv)
    dotted = start_all(dots_ref, hslots, hsems, peers)
    sent = []
    for o, peer in enumerate(low_peers):
        copy = remote(part_ref.at[:, lax.rem(low + 1 + o, LOW)], slots.at[o], gsems, o, peer)
        copy.start()
        sent.append(copy)
    tokens = key_ref.shape[0]
    upper = pl.ds(0, TILE)
    lower = pl.ds(TILE, tokens - TILE)
    moved = [
        remote(next_ref.at[0], from_ref.at[0, 0], wsems, 0, after),
        remote(prev_ref.at[0], from_ref.at[1, 0], wsems, 1, before),
        remote(next_ref.at[1, upper], from_ref.at[0, 1, upper], wsems, 4, after),
        remote(prev_ref.at[1, upper], from_ref.at[1, 1, upper], wsems, 5, before),
        remote(next_ref.at[1, lower], from_ref.at[0, 1, lower], wsems, 6, after),
        remote(prev_ref.at[1, lower], from_ref.at[1, 1, lower], wsems, 7, before),
    ]
    for copy in moved[:2]:
        copy.start()
    total = add_arrivals(dots_ref[...], hslots, dotted)
    total_buf[...] = total
    tot_ref[...] = total
    near = [
        remote(total_buf, near_buf.at[0], wsems, 2, after),
        remote(total_buf, near_buf.at[1], wsems, 3, before),
    ]
    for copy in near:
        copy.start()
    raw = own_tokens(ids_ref, lax.axis_index("ctx") * tokens, key_ref, key_ref) * gain_ref[1:2]
    summed = add_arrivals(part_ref[:, low].astype(jnp.float32), slots, sent)
    each = ZN * G_DEV
    for row in range(yn):
        half[row, 0:each] = summed[0, row * each : (row + 1) * each]
        half[row, each : 2 * each] = summed[1, row * each : (row + 1) * each]
    ysent = []
    for o, peer in enumerate(y_peers):
        copy = remote(half.at[lax.rem(y + 1 + o, yn)], yslots.at[o], gsems, LOW - 1 + o, peer)
        copy.start()
        ysent.append(copy)
    row = add_arrivals(half[y], yslots, ysent)
    quarter[...] = row
    swap = remote(quarter, zslot, gsems, LOW - 1 + yn - 1, other_z)
    for copy in [swap] + moved[2:]:
        copy.start()
    swap.wait_recv()
    reduced = row + zslot[...]
    sum_ref[...] = reduced
    share = jnp.sum(reduced[0:each] * raw, axis=1, keepdims=True)
    extra = jnp.broadcast_to(jnp.concatenate([share, share]), extra_buf.shape)
    extra_buf[...] = extra
    extras = start_all(extra_buf, eslots, esems, peers)
    extra_ref[...] = add_arrivals(extra, eslots, extras)
    for copy in near:
        copy.wait()
    near_ref[...] = near_buf[...]
    for copy in moved:
        copy.wait()
    for copy in sent + ysent + [swap] + dotted + extras:
        copy.wait_send()


def collect(ids, to_prev, to_next, parts, dots, key_raw, gains):
    count = lax.axis_size("ctx")
    heads = lax.axis_size("head")
    yn = count // (LOW * ZN)
    width = parts.shape[-1]
    rows = 2 * ZN * G_DEV
    copies = LOW - 1 + yn
    vmem = pl.BlockSpec(memory_space=pltpu.VMEM)
    free = pl.BlockSpec(memory_space=pl.ANY)
    return pl.pallas_call(
        functools.partial(collect_kernel, count, heads),
        out_shape=(
            jax.ShapeDtypeStruct((2,) + to_prev.shape, jnp.bfloat16),
            jax.ShapeDtypeStruct((rows, width), jnp.float32),
            jax.ShapeDtypeStruct(dots.shape, jnp.float32),
            jax.ShapeDtypeStruct((2,) + dots.shape, jnp.float32),
            jax.ShapeDtypeStruct((rows, 128), jnp.float32),
        ),
        in_specs=[pl.BlockSpec(memory_space=pltpu.SMEM), free, free, vmem, vmem, vmem, vmem],
        out_specs=(free, vmem, vmem, vmem, vmem),
        scratch_shapes=[
            pltpu.VMEM((LOW - 1, 2) + parts.shape[2:], jnp.bfloat16),
            pltpu.VMEM((yn, rows, width), jnp.float32),
            pltpu.VMEM((yn - 1, rows, width), jnp.float32),
            pltpu.VMEM((rows, width), jnp.float32),
            pltpu.VMEM((rows, width), jnp.float32),
            pltpu.VMEM((heads - 1,) + dots.shape, jnp.float32),
            pltpu.VMEM(dots.shape, jnp.float32),
            pltpu.VMEM((2,) + dots.shape, jnp.float32),
            pltpu.VMEM((rows, 128), jnp.float32),
            pltpu.VMEM((heads - 1, rows, 128), jnp.float32),
            pltpu.SemaphoreType.DMA((8,)),
            pltpu.SemaphoreType.DMA((8,)),
            pltpu.SemaphoreType.DMA((copies,)),
            pltpu.SemaphoreType.DMA((copies,)),
            pltpu.SemaphoreType.DMA((heads - 1,)),
            pltpu.SemaphoreType.DMA((heads - 1,)),
            pltpu.SemaphoreType.DMA((heads - 1,)),
            pltpu.SemaphoreType.DMA((heads - 1,)),
        ],
        compiler_params=pltpu.CompilerParams(collective_id=2, has_side_effects=True),
    )(ids, to_prev, to_next, parts, dots, key_raw, gains)


def attention_kernel(
    tiles_ref, readers_ref, tot_ref, near_ref, gain_ref,
    q_ref, g_ref, key_ref, val_ref, win_ref, glob_ref,
    dq_ref, prev_ref, next_ref, own_ref, dglob_ref, dots_ref,
    inverses, queries, keys, vals, dkeys, dvals, dot_sums, live_buf,
):
    tokens = q_ref.shape[0]
    span = KEYS * TILE
    factor = HEAD_DIM ** (-0.5)

    @pl.when(pl.program_id(0) == 0)
    def _():
        own = lax.rsqrt(tot_ref[...] / D + EPSILON)
        near = lax.rsqrt(near_ref[...] / D + EPSILON)
        lines = [own[0:1], own[1:2], near[0, 2:3], near[0, 3:4]]
        lines += [own[2:3], own[3:4], near[1, 2:3], near[1, 3:4]]
        for index, line in enumerate(lines):
            inverses[index * TILE : (index + 1) * TILE] = jnp.broadcast_to(line, (TILE, TILE)).T
        dot_sums[...] = jnp.zeros_like(dot_sums)
        devices = readers_ref.shape[1]
        globals_here = glob_ref.shape[1]
        owner = lax.broadcasted_iota(jnp.int32, (devices, globals_here), 0)
        place = lax.broadcasted_iota(jnp.int32, (devices, globals_here), 1) // G_DEV
        groups = devices // LOW
        match = (owner % LOW == place // groups) & (owner // LOW == place % groups)
        flags = jnp.broadcast_to((readers_ref[...] > 0).astype(jnp.float32), (8, devices))
        live_buf[...] = dot(
            flags.astype(jnp.bfloat16), match.astype(jnp.float32).astype(jnp.bfloat16), ROWS
        )

    qgain = gain_ref[0:1]
    kgain = gain_ref[1:2]
    first_tile = (lax.axis_index("ctx") - 1) * (tokens // TILE)
    last_start = 3 * (tokens // TILE) - KEYS
    query_rows = q_ref[...].astype(jnp.float32)
    queries[...] = (query_rows * inverses[0:tokens] * qgain).astype(jnp.bfloat16)
    blocks = [win_ref[0, 0], key_ref[...], win_ref[1, 0]]
    for index, block in enumerate(blocks):
        rows = slice(index * tokens, (index + 1) * tokens)
        scale = inverses[(index + 1) * tokens : (index + 2) * tokens]
        keys[rows] = (block.astype(jnp.float32) * scale * kgain).astype(jnp.bfloat16)
    vals[0:tokens] = win_ref[0, 1]
    vals[tokens : 2 * tokens] = val_ref[...]
    vals[2 * tokens :] = win_ref[1, 1]
    dkeys[...] = jnp.zeros_like(dkeys)
    dvals[...] = jnp.zeros_like(dvals)
    gkeys = glob_ref[0]
    gvals = glob_ref[1]
    live = live_buf[0:1] > 0
    gdk = 0.0
    gdv = 0.0
    for tile in range(tokens // TILE):
        rows = slice(tile * TILE, (tile + 1) * TILE)
        start = jnp.clip(tiles_ref[tile, 0] - first_tile, 0, last_start)
        window = pl.ds(pl.multiple_of(start * TILE, TILE), span)
        query = queries[rows]
        grad = g_ref[rows]
        wkeys = keys[window]
        wvals = vals[window]
        score_w = dot(query, wkeys, TURNED) * factor
        score_g = jnp.where(live, dot(query, gkeys, TURNED) * factor, -jnp.inf)
        largest = jnp.maximum(
            jnp.max(score_w, axis=1, keepdims=True), jnp.max(score_g, axis=1, keepdims=True)
        )
        exp_w = jnp.exp(score_w - largest)
        exp_g = jnp.exp(score_g - largest)
        inverse = 1.0 / (
            jnp.sum(exp_w, axis=1, keepdims=True) + jnp.sum(exp_g, axis=1, keepdims=True)
        )
        prob_w = exp_w * inverse
        prob_g = exp_g * inverse
        low_w = prob_w.astype(jnp.bfloat16)
        low_g = prob_g.astype(jnp.bfloat16)
        attended = (dot(low_w, wvals, ROWS) + dot(low_g, gvals, ROWS)).astype(jnp.bfloat16)
        delta = jnp.sum(
            grad.astype(jnp.float32) * attended.astype(jnp.float32), axis=1, keepdims=True
        )
        ds_w = (prob_w * (dot(grad, wvals, TURNED) - delta) * factor).astype(jnp.bfloat16)
        ds_g = (prob_g * (dot(grad, gvals, TURNED) - delta) * factor).astype(jnp.bfloat16)
        dq_ref[rows] = dot(ds_w, wkeys, ROWS) + dot(ds_g, gkeys, ROWS)
        dkeys[window] += dot(ds_w, query, DOWN)
        dvals[window] += dot(low_w, grad, DOWN)
        gdk = gdk + dot(ds_g, query, DOWN)
        gdv = gdv + dot(low_g, grad, DOWN)
    for pair_index, cat in enumerate((dkeys, dvals)):
        prev_ref[pair_index] = cat[0:tokens].astype(jnp.bfloat16)
        own_ref[pair_index] = cat[tokens : 2 * tokens]
        next_ref[pair_index] = cat[2 * tokens :].astype(jnp.bfloat16)
    dglob_ref[0] = gdk.astype(jnp.bfloat16)
    dglob_ref[1] = gdv.astype(jnp.bfloat16)
    dot_sums[0:tokens] += dq_ref[...] * qgain * query_rows
    for index, block in enumerate(blocks):
        rows = slice(index * tokens, (index + 1) * tokens)
        dot_sums[(index + 1) * tokens : (index + 2) * tokens] += (
            dkeys[rows] * kgain * block.astype(jnp.float32)
        )

    @pl.when(pl.program_id(0) == pl.num_programs(0) - 1)
    def _():
        for index in range(dots_ref.shape[0]):
            turned = dot_sums[index * TILE : (index + 1) * TILE].T
            dots_ref[index : index + 1] = jnp.sum(turned, axis=0, keepdims=True)


def attention(tiles, readers, totals, near, gains, query, out_grad, key, val, window, globs):
    tokens, width = query.shape
    count = globs.shape[1]
    whole = pl.BlockSpec(memory_space=pltpu.VMEM)
    flat = pl.BlockSpec((tokens, HEAD_DIM), lambda h: (0, h))
    gain = pl.BlockSpec((2, HEAD_DIM), lambda h: (0, h))
    pair = pl.BlockSpec((2, tokens, HEAD_DIM), lambda h: (0, 0, h))
    glob = pl.BlockSpec((2, count, HEAD_DIM), lambda h: (0, 0, h))
    pair_shape = (2, tokens, width)
    lines = 4 * tokens // TILE
    return pl.pallas_call(
        attention_kernel,
        grid=(width // HEAD_DIM,),
        out_shape=(
            jax.ShapeDtypeStruct((tokens, width), jnp.float32),
            jax.ShapeDtypeStruct(pair_shape, jnp.bfloat16),
            jax.ShapeDtypeStruct(pair_shape, jnp.bfloat16),
            jax.ShapeDtypeStruct(pair_shape, jnp.float32),
            jax.ShapeDtypeStruct((2, count, width), jnp.bfloat16),
            jax.ShapeDtypeStruct((lines, TILE), jnp.float32),
        ),
        in_specs=[
            pl.BlockSpec(memory_space=pltpu.SMEM),
            whole,
            whole,
            whole,
            gain,
            flat,
            flat,
            flat,
            flat,
            pl.BlockSpec((2, 2, tokens, HEAD_DIM), lambda h: (0, 0, 0, h)),
            glob,
        ],
        out_specs=(flat, pair, pair, pair, glob, pl.BlockSpec((lines, TILE), lambda h: (0, 0))),
        scratch_shapes=[
            pltpu.VMEM((4 * tokens, HEAD_DIM), jnp.float32),
            pltpu.VMEM((tokens, HEAD_DIM), jnp.bfloat16),
            pltpu.VMEM((3 * tokens, HEAD_DIM), jnp.bfloat16),
            pltpu.VMEM((3 * tokens, HEAD_DIM), jnp.bfloat16),
            pltpu.VMEM((3 * tokens, HEAD_DIM), jnp.float32),
            pltpu.VMEM((3 * tokens, HEAD_DIM), jnp.float32),
            pltpu.VMEM((4 * tokens, HEAD_DIM), jnp.float32),
            pltpu.VMEM((8, count), jnp.float32),
        ],
    )(tiles, readers, totals, near, gains, query, out_grad, key, val, window, globs)


def finish_kernel(
    ids_ref, tot_ref, sum_ref, dots_ref, near_ref, extra_ref, gain_ref,
    q_ref, k_ref, dq_ref, own_ref, from_ref, qg_ref, kg_ref, vg_ref, lines,
):
    tokens = q_ref.shape[0]
    device = lax.axis_index("ctx")
    z = lax.rem(device // LOW, ZN)
    spots = lax.broadcasted_iota(jnp.int32, (tokens, HEAD_DIM), 0) + device * tokens

    @pl.when(pl.program_id(0) == 0)
    def _():
        inverse = lax.rsqrt(tot_ref[...] / D + EPSILON)
        dots = dots_ref[...]
        key_dots = dots[4:6] + near_ref[0, 6:8] + near_ref[1, 2:4]
        rows = [inverse[0:1], inverse[1:2], inverse[2:3], inverse[3:4]]
        rows += [dots[0:1], dots[1:2], key_dots[0:1], key_dots[1:2]]
        for index, row in enumerate(rows):
            lines[index * TILE : (index + 1) * TILE] = jnp.broadcast_to(row, (TILE, TILE)).T
        for index in range(G_DEV):
            extra = jnp.where(z == 0, extra_ref[index : index + 1], extra_ref[G_DEV + index : G_DEV + index + 1])
            lines[3 * tokens :] += jnp.where(spots == ids_ref[index], extra, 0.0)

    home_key = own_ref[0] + from_ref[0, 0].astype(jnp.float32) + from_ref[1, 0].astype(jnp.float32)
    home_val = own_ref[1] + from_ref[0, 1].astype(jnp.float32) + from_ref[1, 1].astype(jnp.float32)
    each = ZN * G_DEV
    for index in range(G_DEV):
        here = spots == ids_ref[index]
        other = G_DEV + index
        add_key = jnp.where(z == 0, sum_ref[index : index + 1], sum_ref[other : other + 1])
        add_val = jnp.where(
            z == 0, sum_ref[each + index : each + index + 1], sum_ref[each + other : each + other + 1]
        )
        home_key = home_key + jnp.where(here, add_key, 0.0)
        home_val = home_val + jnp.where(here, add_val, 0.0)
    query_inv = lines[0:tokens]
    key_inv = lines[tokens : 2 * tokens]
    query_dot = lines[2 * tokens : 3 * tokens]
    key_dot = lines[3 * tokens :]
    qg_ref[...] = (
        query_inv * (gain_ref[0:1] * dq_ref[...])
        - q_ref[...].astype(jnp.float32) * (query_inv * query_inv * query_inv) * (query_dot / D)
    ).astype(jnp.bfloat16)
    kg_ref[...] = (
        key_inv * (gain_ref[1:2] * home_key)
        - k_ref[...].astype(jnp.float32) * (key_inv * key_inv * key_inv) * (key_dot / D)
    ).astype(jnp.bfloat16)
    vg_ref[...] = home_val.astype(jnp.bfloat16)


def finish(ids, totals, reduced, dots, near, extra, gains, query, key, dq, own, arrived):
    tokens, width = query.shape
    whole = pl.BlockSpec(memory_space=pltpu.VMEM)
    flat = pl.BlockSpec((tokens, HEAD_DIM), lambda h: (0, h))

    def rows(count):
        return pl.BlockSpec((count, HEAD_DIM), lambda h: (0, h))

    return pl.pallas_call(
        finish_kernel,
        grid=(width // HEAD_DIM,),
        out_shape=(jax.ShapeDtypeStruct((tokens, width), jnp.bfloat16),) * 3,
        in_specs=[
            pl.BlockSpec(memory_space=pltpu.SMEM),
            whole,
            rows(reduced.shape[0]),
            whole,
            whole,
            whole,
            rows(2),
            flat,
            flat,
            flat,
            pl.BlockSpec((2, tokens, HEAD_DIM), lambda h: (0, 0, h)),
            pl.BlockSpec((2, 2, tokens, HEAD_DIM), lambda h: (0, 0, 0, h)),
        ],
        out_specs=(flat,) * 3,
        scratch_shapes=[pltpu.VMEM((4 * tokens, HEAD_DIM), jnp.float32)],
    )(ids, totals, reduced, dots, near, extra, gains, query, key, dq, own, arrived)


def body(
    query_raw, key_raw, values, out_grad, query_gain, key_gain, key_tiles, global_ids, readers
):
    width = query_raw.shape[1]
    count = lax.axis_size("ctx")
    window, globs, totals, near, gains = spread(
        global_ids, query_raw, key_raw, values, query_gain, key_gain
    )
    globs = (
        globs.reshape(count, 2, G_DEV, width).transpose(1, 0, 2, 3).reshape(2, count * G_DEV, width)
    )
    grad_query, to_prev, to_next, own_grads, glob_grads, dots = attention(
        key_tiles, readers, totals, near, gains, query_raw, out_grad, key_raw, values, window, globs
    )
    parts = glob_grads.reshape(2, LOW, -1, width)
    arrived, reduced, dot_totals, dot_near, extra = collect(
        global_ids, to_prev, to_next, parts, dots, key_raw, gains
    )
    return tuple(finish(
        global_ids, totals, reduced, dot_totals, dot_near, extra, gains,
        query_raw, key_raw, grad_query, own_grads, arrived,
    ))


def solution(mesh):
    return jax.shard_map(
        body,
        mesh=mesh,
        in_specs=(
            P("ctx", "head"),
            P("ctx", "head"),
            P("ctx", "head"),
            P("ctx", "head"),
            P("head"),
            P("head"),
            P("ctx", None),
            P("ctx"),
            P("ctx", None),
        ),
        out_specs=(P("ctx", "head"), P("ctx", "head"), P("ctx", "head")),
        check_vma=False,
    )
```
